32 devices in a mesh: grid: 2 (over x), gx: 4 (over y, core), gy: 4 (over z).
Axes of the slice: x: 2, y: 2, z: 4, core: 2. Of those that a mesh axis runs over, the one named last changes fastest.
Arguments:
- fine_field: float32 [3, 16, 256, 2048], P(None, None, 'gx', ('grid', 'gy')), may hold values from -6 to 6
- fine_previous: float32 [3, 16, 256, 2048], P(None, None, 'gx', ('grid', 'gy')), may hold values from -6 to 6
- fine_speed: float32 [16, 256, 2048], P(None, 'gx', ('grid', 'gy')), may hold values from 0.1 to 0.2
- fine_metric: float32 [16, 256, 2048], P(None, 'gx', ('grid', 'gy')), may hold values from 0.8 to 1.2
- coarse_field: float32 [3, 16, 128, 1024], P(None, None, 'gx', ('grid', 'gy')), may hold values from -6 to 6
- coarse_previous: float32 [3, 16, 128, 1024], P(None, None, 'gx', ('grid', 'gy')), may hold values from -6 to 6
- coarse_speed: float32 [16, 128, 1024], P(None, 'gx', ('grid', 'gy')), may hold values from 0.02 to 0.04
- fine_traction: float32 [256, 2048], P('gx', ('grid', 'gy')), may hold values from 0.4 to 0.8
- coarse_shear: float32 [128, 1024], P('gx', ('grid', 'gy')), may hold values from 1 to 2
Outputs:
- fine_result: float32 [3, 16, 256, 2048], P(None, None, 'gx', ('grid', 'gy'))
- coarse_result: float32 [3, 16, 128, 1024], P(None, None, 'gx', ('grid', 'gy'))
- change_history: float32 [2, 4], replicated
The draws below stay inside these ranges and needn't reach their ends.
All inputs are finite; a program needn't handle non-finite values.
Results may differ from the reference program's by a relative error of at most 0.00002.
Values sent between devices are 32-bit elements; how exact they have to be, the bound alone decides.
No kernel may reach another device: no remote copies, remote signals or barrier semaphores. Data moves between devices by JAX's collectives and lax.ppermute only.
A program may use at most 256 MiB of HBM per device.

```python
import math
import jax
import jax.numpy as jnp
from jax import lax

NZF = 16
NZC = 16
ITERS = 4
STEPS = 2
NX = 256
NY = 2048
MX = 128
MY = 1024


def levels(key, dims, cuts, low, high):
    def one(dim, shards_of):
        draws = jax.random.uniform(jax.random.fold_in(jax.random.fold_in(key, 6), dim), (shards_of,), jnp.float32, low / len(cuts), high / len(cuts))
        return jnp.repeat(jnp.exp(draws), dims[dim] // shards_of).reshape((-1,) + (1,) * (len(dims) - dim - 1))

    level = one(*cuts[0])
    for cut in cuts[1:]:
        level = level * one(*cut)
    return level


def noise(rng, dims, spread, bound, pieces=(), kind=jnp.bfloat16):
    entries = spread * jax.random.normal(rng, dims, jnp.float32)
    if pieces:
        entries = entries * levels(rng, dims, pieces, -0.22, 0.18)
    return jnp.clip(entries, -bound, bound).astype(kind)


def setup_inputs(seed: int = 0) -> dict:
    seeds = jax.random.split(jax.random.key(seed), 10)
    return {
        "fine_field": noise(seeds[0], (3, NZF, NX, NY), 1.0, 6.0, ((2, 4), (3, 8)), jnp.float32),
        "fine_previous": noise(seeds[1], (3, NZF, NX, NY), 1.0, 6.0, ((2, 4), (3, 8)), jnp.float32),
        "fine_speed": jnp.clip(jnp.exp(math.log(0.2) - 0.6931472 * jax.random.uniform(seeds[2], (NZF, NX, NY), jnp.float32) ** levels(seeds[2], (NZF, NX, NY), ((1, 4), (2, 8)), -0.2, 0.2)), 0.1, 0.2),
        "fine_metric": jnp.clip(0.8 + 0.40000004 * jax.random.uniform(seeds[3], (NZF, NX, NY), jnp.float32) ** levels(seeds[3], (NZF, NX, NY), ((1, 4), (2, 8)), -0.2, 0.2), 0.8, 1.2),
        "coarse_field": noise(seeds[4], (3, NZC, MX, MY), 1.0, 6.0, ((2, 4), (3, 8)), jnp.float32),
        "coarse_previous": noise(seeds[5], (3, NZC, MX, MY), 1.0, 6.0, ((2, 4), (3, 8)), jnp.float32),
        "coarse_speed": jnp.clip(jnp.exp(math.log(0.04) - 0.6931472 * jax.random.uniform(seeds[6], (NZC, MX, MY), jnp.float32) ** levels(seeds[6], (NZC, MX, MY), ((1, 4), (2, 8)), -0.2, 0.2)), 0.02, 0.04),
        "fine_traction": jnp.clip(jnp.exp(math.log(0.8) - 0.6931472 * jax.random.uniform(seeds[7], (NX, NY), jnp.float32) ** levels(seeds[7], (NX, NY), ((0, 4), (1, 8)), -0.2, 0.2)), 0.4, 0.8),
        "coarse_shear": jnp.clip(jnp.exp(math.log(2.0) - 0.6931472 * jax.random.uniform(seeds[8], (MX, MY), jnp.float32) ** levels(seeds[8], (MX, MY), ((0, 4), (1, 8)), -0.2, 0.2)), 1.0, 2.0),
    }


def second_diff(padded, along):
    inner = [padded.shape[0], padded.shape[1] - 4, padded.shape[2] - 4, padded.shape[3] - 4]

    def shifted(offset):
        starts = [0, 2, 2, 2]
        starts[along] = 2 + offset
        limits = [starts[index] + inner[index] for index in range(4)]
        return lax.slice(padded, starts, limits)

    return (-shifted(-2) + 16.0 * shifted(-1) - 30.0 * shifted(0) + 16.0 * shifted(1) - shifted(2)) / 12.0


def lateral_diff(plane):
    width_x = plane.shape[1] - 4
    width_y = plane.shape[2] - 4
    center = plane[:, 2:2 + width_x, 2:2 + width_y]
    along_x = (-plane[:, 0:width_x, 2:2 + width_y] + 16.0 * plane[:, 1:1 + width_x, 2:2 + width_y] - 30.0 * center
               + 16.0 * plane[:, 3:3 + width_x, 2:2 + width_y] - plane[:, 4:4 + width_x, 2:2 + width_y]) / 12.0
    along_y = (-plane[:, 2:2 + width_x, 0:width_y] + 16.0 * plane[:, 2:2 + width_x, 1:1 + width_y] - 30.0 * center
               + 16.0 * plane[:, 2:2 + width_x, 3:3 + width_y] - plane[:, 2:2 + width_x, 4:4 + width_y]) / 12.0
    return along_x + along_y


def prolong(values):
    return jnp.repeat(jnp.repeat(values, 2, axis=-2), 2, axis=-1)


def restrict(values):
    shaped = values.reshape(values.shape[:-2] + (values.shape[-2] // 2, 2, values.shape[-1] // 2, 2))
    return (shaped[..., 0, :, 0] + shaped[..., 0, :, 1] + shaped[..., 1, :, 0] + shaped[..., 1, :, 1]) * 0.25


def plane_terms(padded_fine, padded_coarse, speed_bottom, metric_bottom):
    bottom_row = padded_fine.shape[1] - 3
    u_bottom = padded_fine[:, bottom_row, 2:-2, 2:-2]
    fine_higher = padded_fine[:, bottom_row - 1, 2:-2, 2:-2]
    fine_highest = padded_fine[:, bottom_row - 2, 2:-2, 2:-2]
    fine_lateral = lateral_diff(padded_fine[:, bottom_row])
    fine_const = -12.0 * fine_lateral / metric_bottom + fine_highest - 16.0 * fine_higher + 29.0 * u_bottom
    fine_gain = 12.0 / (speed_bottom * metric_bottom)
    fine_base = fine_highest - 8.0 * fine_higher + u_bottom
    coarse_top = padded_coarse[:, 2, 2:-2, 2:-2]
    coarse_next = padded_coarse[:, 3, 2:-2, 2:-2]
    coarse_third = padded_coarse[:, 4, 2:-2, 2:-2]
    coarse_const = lateral_diff(padded_coarse[:, 2]) + (-29.0 * coarse_top + 16.0 * coarse_next - coarse_third) / 12.0
    coarse_base = -coarse_top + 8.0 * coarse_next - coarse_third
    return u_bottom, fine_const, fine_gain, fine_base, coarse_top, coarse_const, coarse_base


def reference(fine_field, fine_previous, fine_speed, fine_metric, coarse_field, coarse_previous, coarse_speed, fine_traction, coarse_shear):
    metric_sq = fine_metric * fine_metric
    widths = ((0, 0), (2, 2), (2, 2), (2, 2))
    history = []
    for step_index in range(STEPS):
        padded_fine = jnp.pad(fine_field, widths)
        padded_coarse = jnp.pad(coarse_field, widths)
        u_bottom, fine_const, fine_gain, fine_base, coarse_top, coarse_const, coarse_base = plane_terms(
            padded_fine, padded_coarse, fine_speed[-1], metric_sq[-1])
        ghost_fine = u_bottom
        ghost_coarse = coarse_top
        changes = []
        for sweep in range(ITERS):
            send_coarse = prolong(coarse_speed[0] * (coarse_const + 14.0 * ghost_coarse / 12.0))
            send_fine = fine_traction * (fine_base + 6.0 * ghost_fine) / 12.0
            next_fine = (fine_gain * send_coarse + fine_const) / 14.0
            next_coarse = (coarse_base - 24.0 * restrict(send_fine) / coarse_shear) / 6.0
            changes.append(jnp.maximum(jnp.max(jnp.abs(next_fine - ghost_fine)), jnp.max(jnp.abs(next_coarse - ghost_coarse))))
            ghost_fine = next_fine
            ghost_coarse = next_coarse
        history.append(jnp.stack(changes))
        bottom_row = NZF + 1
        padded_fine = padded_fine.at[:, bottom_row + 1, 2:-2, 2:-2].set(ghost_fine)
        padded_fine = padded_fine.at[:, bottom_row + 2, 2:-2, 2:-2].set(2.0 * ghost_fine - u_bottom)
        padded_coarse = padded_coarse.at[:, 1, 2:-2, 2:-2].set(ghost_coarse)
        padded_coarse = padded_coarse.at[:, 0, 2:-2, 2:-2].set(2.0 * ghost_coarse - coarse_top)
        fine_change = fine_speed * (second_diff(padded_fine, 2) + second_diff(padded_fine, 3) + metric_sq * second_diff(padded_fine, 1))
        coarse_change = coarse_speed * (second_diff(padded_coarse, 2) + second_diff(padded_coarse, 3) + second_diff(padded_coarse, 1))
        new_fine = 2.0 * fine_field - fine_previous + fine_change
        new_coarse = 2.0 * coarse_field - coarse_previous + coarse_change
        fine_previous = fine_field
        fine_field = new_fine
        coarse_previous = coarse_field
        coarse_field = new_coarse
    return fine_field, coarse_field, jnp.stack(history)
```

```python
import functools

import jax
import jax.numpy as jnp
import numpy as np
from jax import lax
from jax.experimental import pallas as pl
from jax.experimental.pallas import tpu as pltpu
from jax.sharding import PartitionSpec as P

STEPS = 2
LANES = 128
TWELFTH = 1.0 / 12.0
Y = ("grid", "gy")
VMEM_LIMIT = 24 << 20


def turn(x, by, axis):
    return pltpu.roll(x, by % x.shape[axis], axis)


def lateral12(u):
    near = (turn(u, 1, 0) + turn(u, -1, 0)) + (turn(u, 1, 1) + turn(u, -1, 1))
    far = (turn(u, 2, 0) + turn(u, -2, 0)) + (turn(u, 2, 1) + turn(u, -2, 1))
    return 16.0 * near - far - 60.0 * u


def depth12(ref, c, k):
    last = ref.shape[1] - 1

    def tap(offset, weight):
        at = k + offset
        inside = jnp.logical_and(at >= 0, at <= last)
        return jnp.where(inside, weight, 0.0) * ref[c, jnp.clip(at, 0, last)]

    return (tap(-1, 16.0) + tap(1, 16.0)) + (tap(-2, -1.0) + tap(2, -1.0)) - 30.0 * ref[c, k]


def pack_columns(ref):
    comps, layers, rows, cols = ref.shape
    lane = lax.broadcasted_iota(jnp.int32, (rows, LANES), 1)
    zero = jnp.zeros((rows, LANES), jnp.float32)

    def body(k, carry):
        first, last = carry
        for c in range(comps):
            at = 2 * (c * layers + k)
            here = jnp.logical_and(lane >= at, lane < at + 2)
            first = jnp.where(here, pltpu.roll(ref[c, k, :, :LANES], at, 1), first)
            last = jnp.where(here, pltpu.roll(ref[c, k, :, cols - LANES :], lax.rem(at + 2, LANES), 1), last)
        return first, last

    first, last = lax.fori_loop(0, layers, body, (zero, zero))
    even = lax.rem(lane, 2) == 0
    before = jnp.where(even, -first, 16.0 * turn(first, 1, 1) - first)
    after = jnp.where(even, 16.0 * turn(last, -1, 1) - last, -last)
    return before, after


def pack_rows(ref, c, k):
    rows = ref.shape[2]
    u0, u1 = ref[c, k, 0:1, :], ref[c, k, 1:2, :]
    v0, v1 = ref[c, k, rows - 2 : rows - 1, :], ref[c, k, rows - 1 : rows, :]
    return (-u0, 16.0 * u0 - u1), (16.0 * v1 - v0, -v1)


def pack_all(uf, uc, x_down, x_up, y_down, y_up):
    comps, layers, rows, cols = uf.shape
    crows = uc.shape[2]
    for ref, lo, hi in ((uf, 0, rows), (uc, rows, rows + crows)):
        before, after = pack_columns(ref)
        y_down[lo:hi, :] = before
        y_up[lo:hi, :] = after

    def body(k, _):
        for c in range(comps):
            p = c * layers + k
            for ref, at in ((uf, slice(0, cols)), (uc, slice(cols, None))):
                down, up = pack_rows(ref, c, k)
                for r in range(2):
                    x_down[p, r : r + 1, at] = down[r]
                    x_up[p, r : r + 1, at] = up[r]
        return 0

    lax.fori_loop(0, layers, body, 0)


def pack_kernel(uf, uc, x_down, x_up, y_down, y_up):
    pack_all(uf, uc, x_down, x_up, y_down, y_up)


def main_kernel(uf, pf, sp, me, uc, pc, cs, vf, vc, latf, latc):
    comps, layers = uf.shape[:2]

    def fine(k, _):
        s12 = sp[k] * TWELFTH
        m2 = me[k] * me[k]
        for c in range(comps):
            u = uf[c, k]
            lat = lateral12(u)
            latf[c] = lat
            vf[c, k] = 2.0 * u - pf[c, k] + s12 * (lat + m2 * depth12(uf, c, k))
        return 0

    lax.fori_loop(0, layers, fine, 0)

    def coarse(i, _):
        k = layers - 1 - i
        s12 = cs[k] * TWELFTH
        for c in range(comps):
            u = uc[c, k]
            lat = lateral12(u)
            latc[c] = lat
            vc[c, k] = 2.0 * u - pc[c, k] + s12 * (lat + depth12(uc, c, k))
        return 0

    lax.fori_loop(0, layers, coarse, 0)


def pieces(x):
    a = x.astype(jnp.bfloat16)
    rest = x - a.astype(jnp.float32)
    b = rest.astype(jnp.bfloat16)
    c = (rest - b.astype(jnp.float32)).astype(jnp.bfloat16)
    return jnp.concatenate([a, b, c], axis=-1)


def edges_of(mine, theirs, there):
    return jnp.where(there, theirs, 0.0) - mine


def interface(lf, lc, uf, sp, me, uc, cs, tr, sh, widen, narrow, tall, change, row):
    comps, layers, rows, cols = uf.shape
    crows, ccols = sh.shape
    b = layers - 1

    def stretch(planes):
        wide = jnp.dot(pieces(jnp.concatenate(planes, axis=0)), widen[...], preferred_element_type=jnp.float32)
        n = len(planes) * crows
        for half in range(cols // LANES):
            part = wide[:, half * LANES : (half + 1) * LANES]
            tall[half, pl.ds(0, n, 2), :] = part
            tall[half, pl.ds(1, n, 2), :] = part
        return [
            jnp.concatenate(
                [tall[half, i * rows : (i + 1) * rows, :] for half in range(cols // LANES)], axis=1
            )
            for i in range(len(planes))
        ]

    def rows_of(planes):
        n = len(planes) * crows
        for i, plane in enumerate(planes):
            for half in range(cols // LANES):
                tall[half, i * rows : (i + 1) * rows, :] = plane[:, half * LANES : (half + 1) * LANES]
        return tuple(
            jnp.concatenate([tall[half, pl.ds(start, n, 2), :] for half in range(cols // LANES)], axis=1)
            for start in range(2)
        )

    s, m = sp[b], me[b]
    m2 = m * m
    gain = 1.0 / (s * m2)
    inv_m2 = 1.0 / m2
    cs0 = cs[0]
    inv_sh = 1.0 / sh[...]
    t = tr[...]
    c0 = [uc[c, 0] for c in range(comps)]
    pull = [
        cs0 * (lc[c] - 29.0 * uc[c, 0] + 16.0 * uc[c, 1] - uc[c, 2]) * TWELFTH for c in range(comps)
    ]
    wide = stretch([cs0] + pull + c0)
    alpha = gain * wide[0]
    beta, first, weighted = [], [], []
    for c in range(comps):
        ub, u1, u2 = uf[c, b], uf[c, b - 1], uf[c, b - 2]
        e = u2 - lf[c] * inv_m2 - 16.0 * u1 + 29.0 * ub
        bc = (12.0 * gain * wide[1 + c] + e) * (1.0 / 14.0)
        beta.append(bc)
        first.append(jnp.max(jnp.abs(alpha * wide[1 + comps + c] + bc - ub), axis=0, keepdims=True))
        weighted.append(t * bc)
        weighted.append(t * (u2 - 8.0 * u1 + 7.0 * ub))
        weighted.append(t * (u2 - 8.0 * u1 + ub))
    even_rows, odd_rows = rows_of([t * alpha] + weighted)
    sums = jnp.dot(pieces(even_rows + odd_rows), narrow[...], preferred_element_type=jnp.float32)
    even_rows, odd_rows = rows_of([alpha])
    top = jnp.maximum(even_rows, odd_rows)
    top = jnp.maximum(top, turn(top, -1, 1))
    lane = lax.broadcasted_iota(jnp.int32, top.shape, 1)
    top = jnp.where(lax.rem(lane, 2) == 0, top, 0.0)
    top = jnp.dot(pieces(top), narrow[...], preferred_element_type=jnp.float32)

    def part(i):
        return sums[i * crows : (i + 1) * crows, :]

    rate = part(0) * (0.5 * inv_sh)
    history = [[], [], [], []]
    c3s, c4s = [], []
    for c in range(comps):
        q6 = (8.0 * uc[c, 1] - uc[c, 0] - uc[c, 2]) * (1.0 / 6.0)
        pushed, start, still = part(1 + 3 * c), part(2 + 3 * c), part(3 + 3 * c)
        base = q6 - (still * TWELFTH + 0.5 * pushed) * inv_sh
        c1 = q6 - start * (TWELFTH * inv_sh)
        c2 = base - rate * c0[c]
        c3 = base - rate * c1
        c4 = base - rate * c2
        d1, d2, d3, d4 = (jnp.abs(x) for x in (c1 - c0[c], c2 - c1, c3 - c2, c4 - c3))
        history[0].append(d1)
        history[1].append(jnp.maximum(d2, top * d1))
        history[2].append(jnp.maximum(d3, top * d2))
        history[3].append(jnp.maximum(d4, top * d3))
        c3s.append(c3)
        c4s.append(c4)
    for n in range(4):
        d = jnp.maximum(jnp.maximum(history[n][0], history[n][1]), history[n][2])
        d = jnp.max(d, axis=0, keepdims=True)
        if n == 0:
            f = jnp.maximum(jnp.maximum(first[0], first[1]), first[2])
            for half in range(cols // LANES):
                d = jnp.maximum(d, f[:, half * LANES : (half + 1) * LANES])
        change[row + n : row + n + 1, :] = jnp.broadcast_to(jnp.max(d, axis=1, keepdims=True), (1, LANES))
    wide = stretch(c3s)
    return [alpha * wide[c] + beta[c] for c in range(comps)], c4s


def fix_kernel(
    row,
    vf_in, vc_in, latf, latc, uf, sp, me, uc, cs, tr, sh, widen, narrow, change_in,
    own_xd, own_xu, own_yd, own_yu, got_xd, got_xu, got_yd, got_yu,
    *refs,
):
    repack = len(refs) > 7
    vf, vc, change = refs[:3]
    lf, lc, tall, ycorr = refs[-4:]
    comps, layers, rows, cols = uf.shape
    crows = uc.shape[2]
    x_at, x_n = lax.axis_index("gx"), lax.axis_size("gx")
    y_at, y_n = lax.axis_index(Y), lax.axis_size(Y)
    ycorr[0] = edges_of(own_yu[...], got_yu[...], y_at > 0)
    ycorr[1] = edges_of(own_yd[...], got_yd[...], y_at < y_n - 1)
    change[...] = change_in[...]

    def row_edges(p, at):
        low = edges_of(own_xu[p, :, at], got_xu[p, :, at], x_at > 0)
        high = edges_of(own_xd[p, :, at], got_xd[p, :, at], x_at < x_n - 1)
        return low, high

    def column_edges(p, at, n):
        lane = lax.broadcasted_iota(jnp.int32, (n, LANES), 1)
        low = pltpu.roll(ycorr[0, at, :], lax.rem(LANES - 2 * p, LANES), 1)
        high = pltpu.roll(ycorr[1, at, :], lax.rem(2 * LANES - 2 - 2 * p, LANES), 1)
        return jnp.where(lane < 2, low, 0.0), jnp.where(lane >= LANES - 2, high, 0.0)

    def add_edges(get, put, scale, p, xs, ys, n, width):
        low, high = column_edges(p, ys, n)
        if width == LANES:
            put(slice(0, n), slice(0, width), scale(slice(0, n), slice(0, width), low + high))
        else:
            put(slice(0, n), slice(0, LANES), scale(slice(0, n), slice(0, LANES), low))
            put(slice(0, n), slice(width - LANES, width), scale(slice(0, n), slice(width - LANES, width), high))
        low, high = row_edges(p, xs)
        put(slice(0, 2), slice(0, width), scale(slice(0, 2), slice(0, width), low))
        put(slice(n - 2, n), slice(0, width), scale(slice(n - 2, n), slice(0, width), high))

    fine_x, fine_y = slice(0, cols), slice(0, rows)
    coarse_x, coarse_y = slice(cols, cols + uc.shape[3]), slice(rows, rows + crows)

    for c in range(comps):
        lf[c] = latf[c]
        lc[c] = latc[c]

        def put_f(r, l, x, c=c):
            lf[c, r, l] = lf[c, r, l] + x

        def put_c(r, l, x, c=c):
            lc[c, r, l] = lc[c, r, l] + x

        plain = lambda r, l, x: x
        add_edges(None, put_f, plain, c * layers + layers - 1, fine_x, fine_y, rows, cols)
        add_edges(None, put_c, plain, c * layers, coarse_x, coarse_y, crows, uc.shape[3])

    ghost_f, ghost_c = interface(lf, lc, uf, sp, me, uc, cs, tr, sh, widen, narrow, tall, change, row)

    def all_edges(k, _):
        for c in range(comps):
            p = c * layers + k
            for v, v_in, speed, xs, ys, n, width in (
                (vf, vf_in, sp, fine_x, fine_y, rows, cols),
                (vc, vc_in, cs, coarse_x, coarse_y, crows, uc.shape[3]),
            ):

                def scale(r, l, x, speed=speed):
                    return speed[k, r, l] * TWELFTH * x

                def put(r, l, x, v=v):
                    v[c, k, r, l] = v[c, k, r, l] + x

                add_edges(None, put, scale, p, xs, ys, n, width)
        return 0

    b = layers - 1
    s_last = sp[b] * me[b] * me[b] * TWELFTH
    s_next = sp[b - 1] * me[b - 1] * me[b - 1] * TWELFTH
    for c in range(comps):
        vf[c, b] = vf_in[c, b] + s_last * (14.0 * ghost_f[c] + uf[c, b])
        vf[c, b - 1] = vf_in[c, b - 1] - s_next * ghost_f[c]
        vc[c, 0] = vc_in[c, 0] + cs[0] * TWELFTH * (14.0 * ghost_c[c] + uc[c, 0])
        vc[c, 1] = vc_in[c, 1] - cs[1] * TWELFTH * ghost_c[c]
    lax.fori_loop(0, layers, all_edges, 0)
    if repack:
        pack_all(vf, vc, *refs[3:7])


def spec():
    return pl.BlockSpec(memory_space=pltpu.VMEM)


def here(x):
    return pltpu.with_memory_space_constraint(x, pltpu.VMEM)


def call(kernel, args, outs, scratch=(), alias={}, flops=0):
    return pl.pallas_call(
        kernel,
        out_shape=tuple(outs),
        in_specs=[spec() for _ in args],
        out_specs=tuple(spec() for _ in outs),
        scratch_shapes=list(scratch),
        input_output_aliases=alias,
        cost_estimate=pl.CostEstimate(flops=flops, bytes_accessed=flops, transcendentals=0),
        compiler_params=pltpu.CompilerParams(vmem_limit_bytes=VMEM_LIMIT),
    )(*[here(x) for x in args])


def exchange(parts):
    x_down, x_up, y_down, y_up = parts

    def ring(value, axis, by):
        n = lax.axis_size(axis)
        return lax.ppermute(value, axis, [(i, (i + by) % n) for i in range(n)])

    return (ring(x_down, "gx", -1), ring(x_up, "gx", 1), ring(y_down, Y, -1), ring(y_up, Y, 1))


def largest(value):
    for axis in ("gx", "gy", "grid"):
        n, far = lax.axis_size(axis), 1
        while far < n:
            value = jnp.maximum(value, lax.ppermute(value, axis, [(i, (i + far) % n) for i in range(n)]))
            far *= 2
    return value


def on_device(
    fine_field, fine_previous, fine_speed, fine_metric, coarse_field, coarse_previous, coarse_speed,
    fine_traction, coarse_shear,
):
    f32 = jnp.float32
    comps, layers, rows, cols = fine_field.shape
    crows, ccols = coarse_field.shape[2:]
    fine = pltpu.VMEM(fine_field.shape, f32)
    coarse = pltpu.VMEM(coarse_field.shape, f32)
    edge_outs = [
        pltpu.VMEM((comps * layers, 2, cols + ccols), f32),
        pltpu.VMEM((comps * layers, 2, cols + ccols), f32),
        pltpu.VMEM((rows + crows, LANES), f32),
        pltpu.VMEM((rows + crows, LANES), f32),
    ]
    picks = np.zeros((cols, ccols), np.float32)
    picks[np.arange(cols), np.arange(cols) // 2] = 1.0
    narrow = jnp.asarray(np.tile(picks, (3, 1)), jnp.bfloat16)
    widen = jnp.asarray(np.tile(picks.T, (3, 1)), jnp.bfloat16)
    change = jnp.zeros((4 * STEPS, LANES), f32)
    uf, uc, pf, pc = fine_field, coarse_field, fine_previous, coarse_previous
    mine = call(pack_kernel, (uf, uc), edge_outs)
    for step in range(STEPS):
        theirs = exchange(mine)
        vf, vc, latf, latc = call(
            main_kernel,
            (uf, pf, fine_speed, fine_metric, uc, pc, coarse_speed),
            [fine, coarse, pltpu.VMEM((comps, rows, cols), f32), pltpu.VMEM((comps, crows, ccols), f32)],
            flops=40_000_000,
        )
        more = step < STEPS - 1
        results = call(
            functools.partial(fix_kernel, 4 * step),
            (vf, vc, latf, latc, uf, fine_speed, fine_metric, uc, coarse_speed, fine_traction, coarse_shear)
            + (widen, narrow, change) + tuple(mine) + tuple(theirs),
            [fine, coarse, pltpu.VMEM(change.shape, f32)] + (edge_outs if more else []),
            scratch=[
                pltpu.VMEM((comps, rows, cols), f32),
                pltpu.VMEM((comps, crows, ccols), f32),
                pltpu.VMEM((cols // LANES, 10 * rows, LANES), f32),
                pltpu.VMEM((2, rows + crows, LANES), f32),
            ],
            alias={0: 0, 1: 1},
            flops=20_000_000,
        )
        pf, pc = uf, uc
        uf, uc, change = results[:3]
        mine = results[3:]
    history = largest(change)
    return uf, uc, history[:, 0].reshape(STEPS, 4)


def solution(mesh):
    field = P(None, None, "gx", Y)
    layered = P(None, "gx", Y)
    plane = P("gx", Y)
    return jax.shard_map(
        on_device,
        mesh=mesh,
        in_specs=(field, field, layered, layered, field, field, layered, plane, plane),
        out_specs=(field, field, P()),
        check_vma=False,
    )
```

```python
import functools

import jax
import jax.numpy as jnp
import numpy as np
from jax import lax
from jax.experimental import pallas as pl
from jax.experimental.pallas import tpu as pltpu
from jax.sharding import PartitionSpec as P

STEPS = 2
LANES = 128
TWELFTH = 1.0 / 12.0
Y = ("grid", "gy")
VMEM_LIMIT = 16 << 20
EARLY = 4


def turn(x, by, axis):
    return pltpu.roll(x, by % x.shape[axis], axis)


def lateral12(u):
    near = (turn(u, 1, 0) + turn(u, -1, 0)) + (turn(u, 1, 1) + turn(u, -1, 1))
    far = (turn(u, 2, 0) + turn(u, -2, 0)) + (turn(u, 2, 1) + turn(u, -2, 1))
    return 16.0 * near - far - 60.0 * u


def depth12(ref, c, k):
    last = ref.shape[1] - 1

    def pair(offset):
        taps = [ref[c, k + o] for o in (-offset, offset) if not isinstance(k, int) or 0 <= k + o <= last]
        return taps[0] + taps[1] if len(taps) == 2 else taps[0]

    return 16.0 * pair(1) - pair(2) - 30.0 * ref[c, k]


def layers_do(first, stop, total, body):
    a, b = max(first, 2), min(stop, total - 2)
    for k in range(first, min(stop, 2)):
        body(k)
    if b > a:
        pl.loop(a, b)(body)
    for k in range(max(first, total - 2), stop):
        body(k)


def pack_columns(ref, here, k, first, last):
    comps, layers, rows, cols = ref.shape
    for c in range(comps):
        at = 2 * (c * layers + k)
        inside = jnp.logical_and(here >= at, here < at + 2)
        first = jnp.where(inside, pltpu.roll(ref[c, k, :, :LANES], at, 1), first)
        last = jnp.where(inside, pltpu.roll(ref[c, k, :, cols - LANES :], (at + 2) % LANES, 1), last)
    return first, last


def pack_rows(ref, x_down, x_up, k, at):
    comps, layers, rows, cols = ref.shape
    sub = lax.broadcasted_iota(jnp.int32, (8, cols), 0)
    for c in range(comps):
        p = c * layers + k
        top, bottom = ref[c, k, 0:8, :], ref[c, k, rows - 8 : rows, :]
        down = jnp.where(sub == 1, 16.0 * turn(top, 1, 0), 0.0) - top
        up = jnp.where(sub == 0, 16.0 * turn(bottom, 1, 0), 0.0) - turn(bottom, 2, 0)
        x_down[p, :, at] = down[0:2]
        x_up[p, :, at] = up[0:2]


def pack_all(uf, uc, x_down, x_up, y_down, y_up, ready=None):
    layers, rows, cols = uf.shape[1:]
    crows, ccols = uc.shape[2:]
    for ref, ys, xs in ((uf, (0, rows), (0, cols)), (uc, (rows, rows + crows), (cols, cols + ccols))):
        n = ys[1] - ys[0]
        lane = lax.broadcasted_iota(jnp.int32, (n, LANES), 1)
        first = last = jnp.zeros((n, LANES), jnp.float32)
        for k in range(layers):
            if ready is not None:
                ready(ref is uc, k)
            first, last = pack_columns(ref, lane, k, first, last)
            pack_rows(ref, x_down, x_up, k, slice(*xs))
        even = lax.rem(lane, 2) == 0
        y_down[slice(*ys), :] = jnp.where(even, 0.0, 16.0 * turn(first, 1, 1)) - first
        y_up[slice(*ys), :] = jnp.where(even, 16.0 * turn(last, -1, 1), 0.0) - last


def load_kernel(uf_hbm, uc_hbm, uf, uc, x_down, x_up, y_down, y_up, sem):
    layers = uf.shape[1]
    group = 4
    copies = {}
    for coarse, src, dst in ((False, uf_hbm, uf), (True, uc_hbm, uc)):
        for g in range(0, layers, group):
            at = pl.ds(g, group)
            copies[coarse, g] = pltpu.make_async_copy(
                src.at[:, at], dst.at[:, at], sem.at[int(coarse) * (layers // group) + g // group]
            )
            copies[coarse, g].start()

    def ready(coarse, k):
        if (coarse, k) in copies:
            copies[coarse, k].wait()

    pack_all(uf, uc, x_down, x_up, y_down, y_up, ready)


def fine_plane(uf, pf, s12, m2, c, k):
    u = uf[c, k]
    return 2.0 * u - pf[c, k] + s12 * (lateral12(u) + m2 * depth12(uf, c, k))


def coarse_plane(uc, pc, s12, c, k):
    u = uc[c, k]
    return 2.0 * u - pc[c, k] + s12 * (lateral12(u) + depth12(uc, c, k))


def main_kernel(stop, uf, pf, sp, me, uc, pc, cs, vf, vc):
    comps, layers = uf.shape[:2]

    def fine(k):
        s12, m2 = sp[k] * TWELFTH, me[k] * me[k]
        for c in range(comps):
            vf[c, k] = fine_plane(uf, pf, s12, m2, c, k)

    def coarse(k):
        s12 = cs[k] * TWELFTH
        for c in range(comps):
            vc[c, k] = coarse_plane(uc, pc, s12, c, k)

    layers_do(0, stop, layers, fine)
    layers_do(0, layers, layers, coarse)


class Edges:
    def __init__(self, own, got, ycorr, shapes):
        self.own_xd, self.own_xu, own_yd, own_yu = own
        self.got_xd, self.got_xu, got_yd, got_yu = got
        self.ycorr = ycorr
        (self.layers, rows, cols), (crows, ccols) = shapes
        self.fine = (slice(0, rows), slice(0, cols), rows, cols)
        self.coarse = (slice(rows, rows + crows), slice(cols, cols + ccols), crows, ccols)
        x_at, x_n = lax.axis_index("gx"), lax.axis_size("gx")
        y_at, y_n = lax.axis_index(Y), lax.axis_size(Y)
        self.x_low, self.x_high = x_at > 0, x_at < x_n - 1
        ycorr[0] = jnp.where(y_at > 0, got_yu[...], 0.0) - own_yu[...]
        ycorr[1] = jnp.where(y_at < y_n - 1, got_yd[...], 0.0) - own_yd[...]

    def columns(self, grid, p):
        ys, xs, n, width = grid
        lane = lax.broadcasted_iota(jnp.int32, (n, LANES), 1)
        low = pltpu.roll(self.ycorr[0, ys, :], (LANES - 2 * p) % LANES, 1)
        high = pltpu.roll(self.ycorr[1, ys, :], (2 * LANES - 2 - 2 * p) % LANES, 1)
        low, high = jnp.where(lane < 2, low, 0.0), jnp.where(lane >= LANES - 2, high, 0.0)
        if width == LANES:
            return [(slice(0, LANES), low + high)]
        return [(slice(0, LANES), low), (slice(width - LANES, width), high)]

    def rows(self, grid, p):
        ys, xs, n, width = grid
        low = jnp.where(self.x_low, self.got_xu[p, :, xs], 0.0) - self.own_xu[p, :, xs]
        high = jnp.where(self.x_high, self.got_xd[p, :, xs], 0.0) - self.own_xd[p, :, xs]
        return [(slice(0, 2), low), (slice(n - 2, n), high)]

    def add(self, plane, grid, p, speed=None):
        for lanes, x in self.columns(grid, p):
            x = x if speed is None else x * (speed[:, lanes] * TWELFTH)
            plane[:, lanes] = plane[:, lanes] + x
        for rows, x in self.rows(grid, p):
            x = x if speed is None else x * (speed[rows, :] * TWELFTH)
            plane[rows, :] = plane[rows, :] + x


def pieces(x):
    a = x.astype(jnp.bfloat16)
    rest = x - a.astype(jnp.float32)
    b = rest.astype(jnp.bfloat16)
    c = (rest - b.astype(jnp.float32)).astype(jnp.bfloat16)
    return jnp.concatenate([a, b, c], axis=-1)


def interface(edges, uf, sp, me, uc, cs, tr, sh, widen, narrow, lf, lc, tall):
    comps, layers, rows, cols = uf.shape
    crows, ccols = sh.shape
    b = layers - 1

    for c in range(comps):
        lf[c] = lateral12(uf[c, b])
        lc[c] = lateral12(uc[c, 0])
        edges.add(lf.at[c], edges.fine, c * layers + b)
        edges.add(lc.at[c], edges.coarse, c * layers)

    def stretch(planes):
        wide = jnp.dot(pieces(jnp.concatenate(planes, axis=0)), widen[...], preferred_element_type=jnp.float32)
        n = len(planes) * crows
        for half in range(cols // LANES):
            part = wide[:, half * LANES : (half + 1) * LANES]
            tall[half, pl.ds(0, n, 2), :] = part
            tall[half, pl.ds(1, n, 2), :] = part
        return [
            jnp.concatenate(
                [tall[half, i * rows : (i + 1) * rows, :] for half in range(cols // LANES)], axis=1
            )
            for i in range(len(planes))
        ]

    def rows_of(planes):
        n = len(planes) * crows
        for i, plane in enumerate(planes):
            for half in range(cols // LANES):
                tall[half, i * rows : (i + 1) * rows, :] = plane[:, half * LANES : (half + 1) * LANES]
        return tuple(
            jnp.concatenate([tall[half, pl.ds(start, n, 2), :] for half in range(cols // LANES)], axis=1)
            for start in range(2)
        )

    s, m = sp[b], me[b]
    m2 = m * m
    gain = 1.0 / (s * m2)
    inv_m2 = 1.0 / m2
    cs0 = cs[0]
    inv_sh = 1.0 / sh[...]
    t = tr[...]
    c0 = [uc[c, 0] for c in range(comps)]
    pull = [
        cs0 * (lc[c] - 29.0 * uc[c, 0] + 16.0 * uc[c, 1] - uc[c, 2]) * TWELFTH for c in range(comps)
    ]
    wide = stretch([cs0] + pull + c0)
    alpha = gain * wide[0]
    beta, first, weighted = [], [], []
    for c in range(comps):
        ub, u1, u2 = uf[c, b], uf[c, b - 1], uf[c, b - 2]
        e = u2 - lf[c] * inv_m2 - 16.0 * u1 + 29.0 * ub
        bc = (12.0 * gain * wide[1 + c] + e) * (1.0 / 14.0)
        beta.append(bc)
        first.append(jnp.max(jnp.abs(alpha * wide[1 + comps + c] + bc - ub), axis=0, keepdims=True))
        weighted.append(t * bc)
        weighted.append(t * (u2 - 8.0 * u1 + 7.0 * ub))
        weighted.append(t * (u2 - 8.0 * u1 + ub))
    even_rows, odd_rows = rows_of([t * alpha] + weighted)
    sums = jnp.dot(pieces(even_rows + odd_rows), narrow[...], preferred_element_type=jnp.float32)
    even_rows, odd_rows = rows_of([alpha])
    top = jnp.maximum(even_rows, odd_rows)
    top = jnp.maximum(top, turn(top, -1, 1))
    lane = lax.broadcasted_iota(jnp.int32, top.shape, 1)
    top = jnp.where(lax.rem(lane, 2) == 0, top, 0.0)
    top = jnp.dot(pieces(top), narrow[...], preferred_element_type=jnp.float32)

    def part(i):
        return sums[i * crows : (i + 1) * crows, :]

    rate = part(0) * (0.5 * inv_sh)
    history = [[], [], [], []]
    c3s, c4s = [], []
    for c in range(comps):
        q6 = (8.0 * uc[c, 1] - uc[c, 0] - uc[c, 2]) * (1.0 / 6.0)
        pushed, start, still = part(1 + 3 * c), part(2 + 3 * c), part(3 + 3 * c)
        base = q6 - (still * TWELFTH + 0.5 * pushed) * inv_sh
        c1 = q6 - start * (TWELFTH * inv_sh)
        c2 = base - rate * c0[c]
        c3 = base - rate * c1
        c4 = base - rate * c2
        d1, d2, d3, d4 = (jnp.abs(x) for x in (c1 - c0[c], c2 - c1, c3 - c2, c4 - c3))
        history[0].append(d1)
        history[1].append(jnp.maximum(d2, top * d1))
        history[2].append(jnp.maximum(d3, top * d2))
        history[3].append(jnp.maximum(d4, top * d3))
        c3s.append(c3)
        c4s.append(c4)
    lane = lax.broadcasted_iota(jnp.int32, (1, LANES), 1)
    line = jnp.zeros((1, LANES), jnp.float32)
    for n in range(4):
        d = jnp.maximum(jnp.maximum(history[n][0], history[n][1]), history[n][2])
        d = jnp.max(d, axis=0, keepdims=True)
        if n == 0:
            f = jnp.maximum(jnp.maximum(first[0], first[1]), first[2])
            for half in range(cols // LANES):
                d = jnp.maximum(d, f[:, half * LANES : (half + 1) * LANES])
        line = jnp.where(lane == n, jnp.max(d, axis=1, keepdims=True), line)
    wide = stretch(c3s)
    return [alpha * wide[c] + beta[c] for c in range(comps)], c4s, line[:, 0:4]


def fix_kernel(vf_in, vc_in, uf, sp, me, uc, cs, tr, sh, widen, narrow, *refs):
    own, got = refs[0:4], refs[4:8]
    vf, vc, change = refs[8:11]
    packed = refs[11:15]
    lf, lc, tall, ycorr = refs[15:]
    comps, layers, rows, cols = uf.shape
    edges = Edges(own, got, ycorr, (uf.shape[1:], uc.shape[2:]))
    ghost_f, ghost_c, line = interface(edges, uf, sp, me, uc, cs, tr, sh, widen, narrow, lf, lc, tall)
    change[...] = line
    b = layers - 1
    s_last = sp[b] * me[b] * me[b] * TWELFTH
    s_next = sp[b - 1] * me[b - 1] * me[b - 1] * TWELFTH
    for c in range(comps):
        vf[c, b] = vf_in[c, b] + s_last * (14.0 * ghost_f[c] + uf[c, b])
        vf[c, b - 1] = vf_in[c, b - 1] - s_next * ghost_f[c]
        vc[c, 0] = vc_in[c, 0] + cs[0] * TWELFTH * (14.0 * ghost_c[c] + uc[c, 0])
        vc[c, 1] = vc_in[c, 1] - cs[1] * TWELFTH * ghost_c[c]

    @pl.loop(0, layers)
    def _(k):
        for c in range(comps):
            edges.add(vf.at[c, k], edges.fine, c * layers + k, sp.at[k])
            edges.add(vc.at[c, k], edges.coarse, c * layers + k, cs.at[k])

    pack_all(vf, vc, *packed)


def interface_kernel(uf, sp, me, uc, cs, tr, sh, widen, narrow, *refs):
    own, got = refs[0:4], refs[4:8]
    ghost_f, ghost_c, change = refs[8:11]
    lf, lc, tall, ycorr = refs[11:]
    edges = Edges(own, got, ycorr, (uf.shape[1:], uc.shape[2:]))
    g, c4, line = interface(edges, uf, sp, me, uc, cs, tr, sh, widen, narrow, lf, lc, tall)
    for c in range(uf.shape[0]):
        ghost_f[c] = g[c]
        ghost_c[c] = c4[c]
    change[...] = line


def last_kernel(first, stop, early, gate, uf, pf, sp, me, uc, cs, vf, vc, ghost_f, ghost_c, *refs):
    own, got = refs[0:4], refs[4:8]
    with_coarse = first == 0
    outs = refs[10:12] if not with_coarse else refs[8:10]
    out_f, out_c = outs
    done_f, done_c, ycorr, sem = refs[-4:]
    comps, layers, rows, cols = uf.shape
    b = layers - 1
    edges = Edges(own, got, ycorr, (uf.shape[1:], uc.shape[2:]))

    def copy(k):
        return pltpu.make_async_copy(done_f.at[:, k - first], out_f.at[:, k], sem.at[k - first])

    def copy_coarse():
        return pltpu.make_async_copy(done_c, out_c, sem.at[stop - first])

    def fine(k):
        s12, m2 = sp[k] * TWELFTH, me[k] * me[k]
        for c in range(comps):
            if stop <= early:
                done_f[c, k - first] = vf[c, k]
            else:
                u = uf[c, k]
                z = depth12(uf, c, k)
                if isinstance(k, int) and k == b:
                    z = z + 14.0 * ghost_f[c] + u
                if isinstance(k, int) and k == b - 1:
                    z = z - ghost_f[c]
                done_f[c, k - first] = 2.0 * u - pf[c, k] + s12 * (lateral12(u) + m2 * z)
            edges.add(done_f.at[c, k - first], edges.fine, c * layers + k, sp.at[k])
        copy(k).start()

    layers_do(first, stop, layers, fine)
    if with_coarse:

        @pl.loop(0, layers)
        def _(k):
            for c in range(comps):
                done_c[c, k] = vc[c, k]
                edges.add(done_c.at[c, k], edges.coarse, c * layers + k, cs.at[k])

        for c in range(comps):
            done_c[c, 0] = done_c[c, 0] + cs[0] * TWELFTH * (14.0 * ghost_c[c] + uc[c, 0])
            done_c[c, 1] = done_c[c, 1] - cs[1] * TWELFTH * ghost_c[c]
        copy_coarse().start()
    for k in range(first, stop):
        copy(k).wait()
    if with_coarse:
        copy_coarse().wait()


def call(kernel, args, outs, scratch=(), alias={}, flops=0, hbm=()):
    spaces = [pltpu.HBM if i in hbm else pltpu.VMEM for i in range(len(args))]
    return pl.pallas_call(
        kernel,
        out_shape=tuple(outs),
        in_specs=[pl.BlockSpec(memory_space=s) for s in spaces],
        out_specs=tuple(pl.BlockSpec(memory_space=o.memory_space) for o in outs),
        scratch_shapes=list(scratch),
        input_output_aliases=alias,
        cost_estimate=pl.CostEstimate(flops=flops, bytes_accessed=flops, transcendentals=0),
        compiler_params=pltpu.CompilerParams(vmem_limit_bytes=VMEM_LIMIT),
    )(*[pltpu.with_memory_space_constraint(x, s) for x, s in zip(args, spaces)])


def exchange(parts):
    x_down, x_up, y_down, y_up = parts

    def ring(value, axis, by):
        n = lax.axis_size(axis)
        return lax.ppermute(value, axis, [(i, (i + by) % n) for i in range(n)])

    return (ring(x_down, "gx", -1), ring(x_up, "gx", 1), ring(y_down, Y, -1), ring(y_up, Y, 1))


def rounds():
    found = []
    for axis in ("gx", "gy", "grid"):
        n, far = lax.axis_size(axis), 1
        while far < n:
            pairs = [(i, i ^ far) if n & (n - 1) == 0 else (i, (i + far) % n) for i in range(n)]
            found.append((axis, pairs))
            far *= 2
    return found


def on_device(
    fine_field, fine_previous, fine_speed, fine_metric, coarse_field, coarse_previous, coarse_speed,
    fine_traction, coarse_shear,
):
    f32 = jnp.float32
    comps, layers, rows, cols = fine_field.shape
    crows, ccols = coarse_field.shape[2:]
    fine = pltpu.VMEM(fine_field.shape, f32)
    coarse = pltpu.VMEM(coarse_field.shape, f32)
    plane_f = pltpu.VMEM((comps, rows, cols), f32)
    plane_c = pltpu.VMEM((comps, crows, ccols), f32)
    line = pltpu.VMEM((1, 4), f32)
    corrections = pltpu.VMEM((2, rows + crows, LANES), f32)
    edge_outs = [
        pltpu.VMEM((comps * layers, 2, cols + ccols), f32),
        pltpu.VMEM((comps * layers, 2, cols + ccols), f32),
        pltpu.VMEM((rows + crows, LANES), f32),
        pltpu.VMEM((rows + crows, LANES), f32),
    ]
    solve_scratch = [plane_f, plane_c, pltpu.VMEM((cols // LANES, 10 * rows, LANES), f32), corrections]
    picks = np.zeros((cols, ccols), np.float32)
    picks[np.arange(cols), np.arange(cols) // 2] = 1.0
    narrow = jnp.asarray(np.tile(picks, (3, 1)), jnp.bfloat16)
    widen = jnp.asarray(np.tile(picks.T, (3, 1)), jnp.bfloat16)
    sp, me, cs = fine_speed, fine_metric, coarse_speed
    fixed = (fine_traction, coarse_shear, widen, narrow)

    uf, uc, *mine = call(
        load_kernel, (fine_field, coarse_field), [fine, coarse] + edge_outs,
        scratch=[pltpu.SemaphoreType.DMA((2 * layers // 4,))], hbm=(0, 1),
    )
    pf, pc = fine_previous, coarse_previous
    theirs = exchange(mine)
    vf, vc = call(
        functools.partial(main_kernel, layers), (uf, pf, sp, me, uc, pc, cs), [fine, coarse], flops=40_000_000
    )
    vf, vc, change0, *ours = call(
        fix_kernel,
        (vf, vc, uf, sp, me, uc, cs) + fixed + (*mine, *theirs),
        [fine, coarse, line] + edge_outs, scratch=solve_scratch, alias={0: 0, 1: 1}, flops=20_000_000,
    )
    pf, pc, uf, uc, mine = uf, uc, vf, vc, ours
    theirs = exchange(mine)
    vf, vc = call(
        functools.partial(main_kernel, EARLY), (uf, pf, sp, me, uc, pc, cs), [fine, coarse], flops=20_000_000
    )
    ghost_f, ghost_c, change1 = call(
        interface_kernel,
        (uf, sp, me, uc, cs) + fixed + (*mine, *theirs),
        [plane_f, plane_c, line], scratch=solve_scratch, flops=10_000_000,
    )
    history = jnp.concatenate([change0, change1], axis=0)
    steps = rounds()
    bounds = [0, EARLY] + [EARLY + (layers - EARLY) * (i + 1) // 4 for i in range(4)]
    outs = ()
    for i in range(max(len(steps), len(bounds) - 1)):
        if i < len(steps):
            axis, pairs = steps[i]
            arrived = lax.ppermute(history, axis, pairs)
        if i < len(bounds) - 1:
            first, stop = bounds[i : i + 2]
            args = (history, uf, pf, sp, me, uc, cs, vf, vc, ghost_f, ghost_c, *mine, *theirs, *outs)
            n = len(args)
            outs = call(
                functools.partial(last_kernel, first, stop, EARLY), args,
                [pltpu.HBM(fine_field.shape, f32), pltpu.HBM(coarse_field.shape, f32)],
                scratch=[
                    pltpu.VMEM((comps, stop - first, rows, cols), f32), coarse, corrections,
                    pltpu.SemaphoreType.DMA((stop - first + 1,)),
                ],
                alias={n - 2: 0, n - 1: 1} if outs else {}, hbm=(n - 2, n - 1) if outs else (), flops=10_000_000,
            )
        if i < len(steps):
            history = jnp.maximum(history, arrived)
    return outs[0], outs[1], history


def solution(mesh):
    field = P(None, None, "gx", Y)
    layered = P(None, "gx", Y)
    plane = P("gx", Y)
    return jax.shard_map(
        on_device,
        mesh=mesh,
        in_specs=(field, field, layered, layered, field, field, layered, plane, plane),
        out_specs=(field, field, P()),
        check_vma=False,
    )
```

```python
import functools

import jax
import jax.numpy as jnp
import numpy as np
from jax import lax
from jax.experimental import pallas as pl
from jax.experimental.pallas import tpu as pltpu
from jax.sharding import PartitionSpec as P

STEPS = 2
LANES = 128
TWELFTH = 1.0 / 12.0
Y = ("grid", "gy")
VMEM_LIMIT = 16 << 20


def turn(x, by, axis):
    return pltpu.roll(x, by % x.shape[axis], axis)


def bands(length, copies):
    one = sum(w * np.eye(length, k=o) for o, w in ((1, 16.0), (-1, 16.0), (2, -1.0), (-2, -1.0)))
    return np.kron(np.eye(copies), one)


def lateral_tables(rows, cols):
    stack = 256 // rows
    left, right = bands(rows, stack), bands(cols, 1)
    return (
        jnp.asarray(np.concatenate([left, left], axis=1), jnp.bfloat16),
        jnp.asarray(np.concatenate([right, right], axis=0), jnp.bfloat16),
    )


def lateral12(planes, left, right):
    a = planes.astype(jnp.bfloat16)
    b = (planes - a.astype(jnp.float32)).astype(jnp.bfloat16)
    y = jnp.dot(jnp.concatenate([a, b], axis=1), right[...], preferred_element_type=jnp.float32)
    x = jnp.dot(left[...], jnp.concatenate([a, b], axis=0), preferred_element_type=jnp.float32)
    return (x + y) - 60.0 * planes


def depth12(ref, c, k):
    last = ref.shape[1] - 1

    def pair(offset):
        taps = [ref[c, k + o] for o in (-offset, offset) if not isinstance(k, int) or 0 <= k + o <= last]
        return taps[0] + taps[1] if len(taps) == 2 else taps[0]

    return 16.0 * pair(1) - pair(2) - 30.0 * ref[c, k]


def slot(p):
    return (p // 32) * LANES + (p % 32) * 4


def column_tables(planes):
    pack, unpack = np.zeros((2 * LANES, 2 * LANES)), np.zeros((2 * LANES, 2 * LANES))
    for p in range(planes):
        v0, v1, u0, u1 = (slot(p) + i for i in range(4))
        down, up = 2 * p, LANES + 2 * p
        pack[u0, down] = -1.0
        pack[u0, down + 1], pack[u1, down + 1] = 16.0, -1.0
        pack[v0, up], pack[v1, up] = -1.0, 16.0
        pack[v1, up + 1] = -1.0
        unpack[2 * p, slot(p) + 2] = unpack[2 * p + 1, slot(p) + 3] = 1.0
        unpack[LANES + 2 * p, slot(p)] = unpack[LANES + 2 * p + 1, slot(p) + 1] = 1.0
    return tuple(jnp.asarray(np.tile(t, (3, 1)), jnp.bfloat16) for t in (pack, unpack))


def pieces(x):
    a = x.astype(jnp.bfloat16)
    rest = x - a.astype(jnp.float32)
    b = rest.astype(jnp.bfloat16)
    c = (rest - b.astype(jnp.float32)).astype(jnp.bfloat16)
    return jnp.concatenate([a, b, c], axis=-1)


def times(x, table):
    return jnp.dot(pieces(x), table[...], preferred_element_type=jnp.float32)


def pack_all(uf, uc, pack, x_down, x_up, y_down, y_up, ready=None, ready_table=None):
    comps, layers, rows, cols = uf.shape
    crows, ccols = uc.shape[2:]
    raw = []
    for ref, at in ((uf, slice(0, cols)), (uc, slice(cols, cols + ccols))):
        n, width = ref.shape[2:]
        lane = lax.broadcasted_iota(jnp.int32, (n, LANES), 1)
        sub = lax.broadcasted_iota(jnp.int32, (8, width), 0)
        columns = [jnp.zeros((n, LANES), jnp.float32) for _ in range(2)]
        for g in range(0, layers, 4):
            if ready is not None:
                ready(ref is uc, g)
            for c in range(comps):
                first = last = jnp.zeros((8, width), jnp.float32)
                for i in range(4):
                    p = c * layers + g + i
                    u = ref[c, g + i, :, 0:LANES]
                    if width > LANES:
                        u = jnp.where(lane < 2, u, ref[c, g + i, :, width - LANES : width])
                    u = turn(u, slot(p) % LANES + 2, 1)
                    half = slot(p) // LANES
                    columns[half] = jnp.where(lane // 4 == slot(p) % LANES // 4, u, columns[half])
                    first = jnp.where(sub // 2 == i, turn(ref[c, g + i, 0:8, :], 2 * i, 0), first)
                    last = jnp.where(sub // 2 == i, turn(ref[c, g + i, n - 8 : n, :], 2 * i + 2, 0), last)
                tile = (c * layers + g) // 4
                x_down[tile, :, at] = jnp.where(lax.rem(sub, 2) == 1, 16.0 * turn(first, 1, 0), 0.0) - first
                x_up[tile, :, at] = jnp.where(lax.rem(sub, 2) == 0, 16.0 * turn(last, -1, 0), 0.0) - last
        raw.append(jnp.concatenate(columns, axis=1))
    if ready_table is not None:
        ready_table()
    packed = times(jnp.concatenate(raw, axis=0), pack)
    y_down[...] = packed[:, 0:LANES]
    y_up[...] = packed[:, LANES : 2 * LANES]


def load_kernel(uf_hbm, uc_hbm, pack_hbm, uf, uc, x_down, x_up, y_down, y_up, pack, sem):
    layers = uf.shape[1]
    copies = {}
    for coarse, src, dst in ((False, uf_hbm, uf), (True, uc_hbm, uc)):
        for g in range(0, layers, 4):
            at = pl.ds(g, 4)
            copies[coarse, g] = pltpu.make_async_copy(src.at[:, at], dst.at[:, at], sem.at[int(coarse), g // 4])
            copies[coarse, g].start()
    table = pltpu.make_async_copy(pack_hbm, pack, sem.at[2, 0])
    table.start()

    def ready(coarse, g):
        copies[coarse, g].wait()

    pack_all(uf, uc, pack, x_down, x_up, y_down, y_up, ready, table.wait)


def groups_do(total, size, body):
    body(0)
    if total > 2 * size:

        @pl.loop(1, total // size - 1)
        def _(g):
            body(g * size)

    body(total - size)


def main_kernel(fetch, uf, pf_in, sp, me, uc, pc, cs, left_f, right_f, left_c, right_c, vf, vc, lat, *rest):
    comps, layers, rows, cols = uf.shape
    crows, ccols = uc.shape[2:]
    size_f, size_c = 256 // rows, 256 // crows
    pf = pf_in
    if fetch:
        pf, sem = rest

        def copy(k):
            at = pl.ds(k, size_f)
            return pltpu.make_async_copy(pf_in.at[:, at], pf.at[:, at], sem.at[k // size_f])

        for k in range(0, layers, size_f):
            copy(k).start()

    def coarse(first):
        for c in range(comps):
            planes = uc[c, pl.ds(first, size_c)].reshape(256, ccols)
            part = lateral12(planes, left_c, right_c)
            for i in range(size_c):
                k = first + i
                total = part[i * crows : (i + 1) * crows, :] + depth12(uc, c, k)
                vc[c, k] = 2.0 * uc[c, k] - pc[c, k] + cs[k] * TWELFTH * total

    def fine(first):
        for c in range(comps):
            planes = uf[c, pl.ds(first, size_f)].reshape(256, cols)
            lat[c] = lateral12(planes, left_f, right_f)
        if fetch:
            copy(first).wait()
        for i in range(size_f):
            k = first + i
            s12, m2 = sp[k] * TWELFTH, me[k] * me[k]
            for c in range(comps):
                total = lat[c, i * rows : (i + 1) * rows, :] + m2 * depth12(uf, c, k)
                vf[c, k] = 2.0 * uf[c, k] - pf[c, k] + s12 * total

    groups_do(layers, size_c, coarse)
    groups_do(layers, size_f, fine)


class Edges:
    def __init__(self, got, unpack, slots, shapes):
        self.got_xd, self.got_xu, got_yd, got_yu = got
        self.slots = slots
        (self.layers, rows, cols), (crows, ccols) = shapes
        self.fine = (slice(0, rows), slice(0, cols), rows, cols)
        self.coarse = (slice(rows, rows + crows), slice(cols, cols + ccols), crows, ccols)
        x_at, x_n = lax.axis_index("gx"), lax.axis_size("gx")
        y_at, y_n = lax.axis_index(Y), lax.axis_size(Y)
        self.x_low, self.x_high = x_at > 0, x_at < x_n - 1
        up = jnp.where(y_at > 0, got_yu[...], 0.0)
        down = jnp.where(y_at < y_n - 1, got_yd[...], 0.0)
        both = times(jnp.concatenate([up, down], axis=1), unpack)
        slots[0] = both[:, 0:LANES]
        slots[1] = both[:, LANES : 2 * LANES]

    def plane(self, grid, c, g, i):
        ys, xs, n, width = grid
        p = c * self.layers + g + i
        lane = lax.broadcasted_iota(jnp.int32, (n, LANES), 1)
        sub = lax.broadcasted_iota(jnp.int32, (8, width), 0)
        half, quad = (p // 32, p % 32) if isinstance(p, int) else (lax.div(p, 32), lax.rem(p, 32))
        u = pltpu.roll(self.slots[half, ys, :], LANES - 2 - 4 * quad, 1)
        low, high = jnp.where(lane < 2, u, 0.0), jnp.where(lane >= LANES - 2, u, 0.0)
        if width == LANES:
            columns = low + high
        else:
            columns = jnp.concatenate([low, high], axis=1)
        tile = p // 4 if isinstance(p, int) else lax.div(c * self.layers + g, 4)
        first = jnp.where(jnp.logical_and(sub < 2, self.x_low), turn(self.got_xu[tile, :, xs], -2 * i, 0), 0.0)
        last = jnp.where(jnp.logical_and(sub >= 6, self.x_high), turn(self.got_xd[tile, :, xs], 6 - 2 * i, 0), 0.0)
        return jnp.concatenate([columns[0:8] + first, columns[8 : n - 8], columns[n - 8 : n] + last], axis=0)


def interface(edges, uf, sp, me, uc, cs, tr, sh, widen, narrow, tables, tall):
    comps, layers, rows, cols = uf.shape
    crows, ccols = sh.shape
    b = layers - 1

    left_f, right_f, left_c, right_c = tables
    some = jnp.concatenate([uf[i % comps, b] for i in range(256 // rows)], axis=0)
    lat_f = lateral12(some, left_f, right_f)
    some = jnp.concatenate([uc[i % comps, 0] for i in range(256 // crows)], axis=0)
    lat_c = lateral12(some, left_c, right_c)
    lf, lc = [], []
    for c in range(comps):
        lf.append(lat_f[c * rows : (c + 1) * rows, :] + edges.plane(edges.fine, c, b - 3, 3))
        lc.append(lat_c[c * crows : (c + 1) * crows, :] + edges.plane(edges.coarse, c, 0, 0))

    def stretch(planes):
        wide = times(jnp.concatenate(planes, axis=0), widen)
        n = len(planes) * crows
        for half in range(cols // LANES):
            part = wide[:, half * LANES : (half + 1) * LANES]
            tall[half, pl.ds(0, n, 2), :] = part
            tall[half, pl.ds(1, n, 2), :] = part
        return [
            jnp.concatenate(
                [tall[half, i * rows : (i + 1) * rows, :] for half in range(cols // LANES)], axis=1
            )
            for i in range(len(planes))
        ]

    def rows_of(planes):
        n = len(planes) * crows
        for i, plane in enumerate(planes):
            for half in range(cols // LANES):
                tall[half, i * rows : (i + 1) * rows, :] = plane[:, half * LANES : (half + 1) * LANES]
        return tuple(
            jnp.concatenate([tall[half, pl.ds(start, n, 2), :] for half in range(cols // LANES)], axis=1)
            for start in range(2)
        )

    s, m = sp[b], me[b]
    m2 = m * m
    gain = 1.0 / (s * m2)
    inv_m2 = 1.0 / m2
    cs0 = cs[0]
    inv_sh = 1.0 / sh[...]
    t = tr[...]
    c0 = [uc[c, 0] for c in range(comps)]
    pull = [
        cs0 * (lc[c] - 29.0 * uc[c, 0] + 16.0 * uc[c, 1] - uc[c, 2]) * TWELFTH for c in range(comps)
    ]
    wide = stretch([cs0] + pull + c0)
    alpha = gain * wide[0]
    beta, first, weighted = [], [], []
    for c in range(comps):
        ub, u1, u2 = uf[c, b], uf[c, b - 1], uf[c, b - 2]
        e = u2 - lf[c] * inv_m2 - 16.0 * u1 + 29.0 * ub
        bc = (12.0 * gain * wide[1 + c] + e) * (1.0 / 14.0)
        beta.append(bc)
        first.append(jnp.max(jnp.abs(alpha * wide[1 + comps + c] + bc - ub), axis=0, keepdims=True))
        weighted.append(t * bc)
        weighted.append(t * (u2 - 8.0 * u1 + 7.0 * ub))
        weighted.append(t * (u2 - 8.0 * u1 + ub))
    even_rows, odd_rows = rows_of([t * alpha] + weighted)
    sums = times(even_rows + odd_rows, narrow)
    even_rows, odd_rows = rows_of([alpha])
    top = jnp.maximum(even_rows, odd_rows)
    top = jnp.maximum(top, turn(top, -1, 1))
    lane = lax.broadcasted_iota(jnp.int32, top.shape, 1)
    top = jnp.where(lax.rem(lane, 2) == 0, top, 0.0)
    top = times(top, narrow)

    def part(i):
        return sums[i * crows : (i + 1) * crows, :]

    rate = part(0) * (0.5 * inv_sh)
    history = [[], [], [], []]
    c3s, c4s = [], []
    for c in range(comps):
        q6 = (8.0 * uc[c, 1] - uc[c, 0] - uc[c, 2]) * (1.0 / 6.0)
        pushed, start, still = part(1 + 3 * c), part(2 + 3 * c), part(3 + 3 * c)
        base = q6 - (still * TWELFTH + 0.5 * pushed) * inv_sh
        c1 = q6 - start * (TWELFTH * inv_sh)
        c2 = base - rate * c0[c]
        c3 = base - rate * c1
        c4 = base - rate * c2
        d1, d2, d3, d4 = (jnp.abs(x) for x in (c1 - c0[c], c2 - c1, c3 - c2, c4 - c3))
        history[0].append(d1)
        history[1].append(jnp.maximum(d2, top * d1))
        history[2].append(jnp.maximum(d3, top * d2))
        history[3].append(jnp.maximum(d4, top * d3))
        c3s.append(c3)
        c4s.append(c4)
    lane = lax.broadcasted_iota(jnp.int32, (1, LANES), 1)
    line = jnp.zeros((1, LANES), jnp.float32)
    for n in range(4):
        d = jnp.maximum(jnp.maximum(history[n][0], history[n][1]), history[n][2])
        d = jnp.max(d, axis=0, keepdims=True)
        if n == 0:
            f = jnp.maximum(jnp.maximum(first[0], first[1]), first[2])
            for half in range(cols // LANES):
                d = jnp.maximum(d, f[:, half * LANES : (half + 1) * LANES])
        line = jnp.where(lane == n, jnp.max(d, axis=1, keepdims=True), line)
    wide = stretch(c3s)
    return [alpha * wide[c] + beta[c] for c in range(comps)], c4s, line[:, 0:4]


def fix_kernel(vf_in, vc_in, pack, uf, sp, me, uc, cs, tr, sh, widen, narrow, *refs):
    tables, unpack, got = refs[0:4], refs[4], refs[5:9]
    vf, vc, change = refs[9:12]
    packed = refs[12:16]
    tall, slots = refs[16:]
    comps, layers, rows, cols = uf.shape
    edges = Edges(got, unpack, slots, (uf.shape[1:], uc.shape[2:]))
    ghost_f, ghost_c, line = interface(edges, uf, sp, me, uc, cs, tr, sh, widen, narrow, tables, tall)
    change[...] = line
    b = layers - 1
    s_last = sp[b] * me[b] * me[b] * TWELFTH
    s_next = sp[b - 1] * me[b - 1] * me[b - 1] * TWELFTH
    for c in range(comps):
        vf[c, b] = vf_in[c, b] + s_last * (14.0 * ghost_f[c] + uf[c, b])
        vf[c, b - 1] = vf_in[c, b - 1] - s_next * ghost_f[c]
        vc[c, 0] = vc_in[c, 0] + cs[0] * TWELFTH * (14.0 * ghost_c[c] + uc[c, 0])
        vc[c, 1] = vc_in[c, 1] - cs[1] * TWELFTH * ghost_c[c]

    @pl.loop(0, layers // 4)
    def _(quarter):
        g = quarter * 4
        for i in range(4):
            s12, cs12 = sp[g + i] * TWELFTH, cs[g + i] * TWELFTH
            for c in range(comps):
                vf[c, g + i] = vf_in[c, g + i] + s12 * edges.plane(edges.fine, c, g, i)
                vc[c, g + i] = vc_in[c, g + i] + cs12 * edges.plane(edges.coarse, c, g, i)

    pack_all(vf, vc, pack, *packed)


def interface_kernel(uf, sp, me, uc, cs, tr, sh, widen, narrow, *refs):
    tables, unpack, got = refs[0:4], refs[4], refs[5:9]
    ghost_f, ghost_c, change = refs[9:12]
    tall, slots = refs[12:]
    edges = Edges(got, unpack, slots, (uf.shape[1:], uc.shape[2:]))
    g, c4, line = interface(edges, uf, sp, me, uc, cs, tr, sh, widen, narrow, tables, tall)
    for c in range(uf.shape[0]):
        ghost_f[c] = g[c]
        ghost_c[c] = c4[c]
    change[...] = line


def last_kernel(first, stop, gate, sp, me, cs, uf, uc, vf, vc, ghost_f, ghost_c, unpack, *refs):
    got = refs[0:4]
    with_coarse = first == 0
    out_f, out_c = refs[4:6] if with_coarse else refs[6:8]
    done_f, done_c, slots, sem = refs[-4:]
    comps, layers, rows, cols = uf.shape
    b = layers - 1
    edges = Edges(got, unpack, slots, (uf.shape[1:], uc.shape[2:]))

    def copy(k):
        return pltpu.make_async_copy(done_f.at[:, k - first], out_f.at[:, k], sem.at[k - first])

    def copy_coarse():
        return pltpu.make_async_copy(done_c, out_c, sem.at[stop - first])

    if with_coarse:

        @pl.loop(0, layers // 4)
        def _(quarter):
            g = quarter * 4
            for i in range(4):
                cs12 = cs[g + i] * TWELFTH
                for c in range(comps):
                    done_c[c, g + i] = vc[c, g + i] + cs12 * edges.plane(edges.coarse, c, g, i)

        for c in range(comps):
            done_c[c, 0] = done_c[c, 0] + cs[0] * TWELFTH * (14.0 * ghost_c[c] + uc[c, 0])
            done_c[c, 1] = done_c[c, 1] - cs[1] * TWELFTH * ghost_c[c]
        copy_coarse().start()
    for g in range(first, stop, 4):
        for i in range(4):
            k = g + i
            s12 = sp[k] * TWELFTH
            for c in range(comps):
                total = edges.plane(edges.fine, c, g, i)
                if k == b:
                    total = total + me[k] * me[k] * (14.0 * ghost_f[c] + uf[c, b])
                if k == b - 1:
                    total = total - me[k] * me[k] * ghost_f[c]
                done_f[c, k - first] = vf[c, k] + s12 * total
            copy(k).start()
    for k in range(first, stop):
        copy(k).wait()
    if with_coarse:
        copy_coarse().wait()


def call(kernel, args, outs, scratch=(), alias={}, flops=0, hbm=()):
    spaces = [pltpu.HBM if i in hbm else pltpu.VMEM for i in range(len(args))]
    return pl.pallas_call(
        kernel,
        out_shape=tuple(outs),
        in_specs=[pl.BlockSpec(memory_space=s) for s in spaces],
        out_specs=tuple(pl.BlockSpec(memory_space=o.memory_space) for o in outs),
        scratch_shapes=list(scratch),
        input_output_aliases=alias,
        cost_estimate=pl.CostEstimate(flops=flops, bytes_accessed=flops, transcendentals=0),
        compiler_params=pltpu.CompilerParams(vmem_limit_bytes=VMEM_LIMIT),
    )(*[pltpu.with_memory_space_constraint(x, s) for x, s in zip(args, spaces)])


def exchange(parts):
    x_down, x_up, y_down, y_up = parts

    def ring(value, axis, by):
        n = lax.axis_size(axis)
        return lax.ppermute(value, axis, [(i, (i + by) % n) for i in range(n)])

    return (ring(x_down, "gx", -1), ring(x_up, "gx", 1), ring(y_down, Y, -1), ring(y_up, Y, 1))


def rounds():
    found = []
    for axis in ("gx", "gy", "grid"):
        n, far = lax.axis_size(axis), 1
        while far < n:
            pairs = [(i, i ^ far) if n & (n - 1) == 0 else (i, (i + far) % n) for i in range(n)]
            found.append((axis, pairs))
            far *= 2
    return found


def on_device(
    fine_field, fine_previous, fine_speed, fine_metric, coarse_field, coarse_previous, coarse_speed,
    fine_traction, coarse_shear,
):
    f32 = jnp.float32
    comps, layers, rows, cols = fine_field.shape
    crows, ccols = coarse_field.shape[2:]
    fine = pltpu.VMEM(fine_field.shape, f32)
    coarse = pltpu.VMEM(coarse_field.shape, f32)
    plane_f = pltpu.VMEM((comps, rows, cols), f32)
    plane_c = pltpu.VMEM((comps, crows, ccols), f32)
    line = pltpu.VMEM((1, 4), f32)
    corrections = pltpu.VMEM((2, rows + crows, LANES), f32)
    edge_outs = [
        pltpu.VMEM((comps * layers // 4, 8, cols + ccols), f32),
        pltpu.VMEM((comps * layers // 4, 8, cols + ccols), f32),
        pltpu.VMEM((rows + crows, LANES), f32),
        pltpu.VMEM((rows + crows, LANES), f32),
    ]
    solve_scratch = [pltpu.VMEM((cols // LANES, 10 * rows, LANES), f32), corrections]
    picks = np.zeros((cols, ccols), np.float32)
    picks[np.arange(cols), np.arange(cols) // 2] = 1.0
    narrow = jnp.asarray(np.tile(picks, (3, 1)), jnp.bfloat16)
    widen = jnp.asarray(np.tile(picks.T, (3, 1)), jnp.bfloat16)
    sp, me, cs = fine_speed, fine_metric, coarse_speed
    tables = (*lateral_tables(rows, cols), *lateral_tables(crows, ccols))
    pack, unpack = column_tables(comps * layers)
    fixed = (fine_traction, coarse_shear, widen, narrow, *tables, unpack)
    lat = pltpu.VMEM((comps, 256, cols), f32)

    uf, uc, *mine = call(
        load_kernel, (fine_field, coarse_field, pack), [fine, coarse] + edge_outs,
        scratch=[pltpu.VMEM(pack.shape, pack.dtype), pltpu.SemaphoreType.DMA((3, layers // 4))], hbm=(0, 1, 2),
    )
    pf, pc = fine_previous, coarse_previous
    theirs = exchange(mine)
    vf, vc = call(
        functools.partial(main_kernel, True), (uf, pf, sp, me, uc, pc, cs, *tables), [fine, coarse],
        scratch=[lat, fine, pltpu.SemaphoreType.DMA((layers,))], hbm=(1,), flops=40_000_000,
    )
    vf, vc, change0, *ours = call(
        fix_kernel,
        (vf, vc, pack, uf, sp, me, uc, cs) + fixed + theirs,
        [fine, coarse, line] + edge_outs, scratch=solve_scratch, alias={0: 0, 1: 1}, flops=20_000_000,
    )
    pf, pc, uf, uc, mine = uf, uc, vf, vc, ours
    theirs = exchange(mine)
    vf, vc = call(
        functools.partial(main_kernel, False), (uf, pf, sp, me, uc, pc, cs, *tables), [fine, coarse],
        scratch=[lat], flops=40_000_000,
    )
    ghost_f, ghost_c, change1 = call(
        interface_kernel,
        (uf, sp, me, uc, cs) + fixed + theirs,
        [plane_f, plane_c, line], scratch=solve_scratch, flops=10_000_000,
    )
    history = jnp.concatenate([change0, change1], axis=0)
    steps = rounds()
    bounds = [0, 4, 8, 12, layers]
    outs = ()
    for i in range(max(len(steps), len(bounds) - 1)):
        if i < len(steps):
            axis, pairs = steps[i]
            arrived = lax.ppermute(history, axis, pairs)
        if i < len(bounds) - 1:
            first, stop = bounds[i : i + 2]
            args = (history, sp, me, cs, uf, uc, vf, vc, ghost_f, ghost_c, unpack, *theirs, *outs)
            n = len(args)
            outs = call(
                functools.partial(last_kernel, first, stop), args,
                [pltpu.HBM(fine_field.shape, f32), pltpu.HBM(coarse_field.shape, f32)],
                scratch=[
                    pltpu.VMEM((comps, stop - first, rows, cols), f32), coarse, corrections,
                    pltpu.SemaphoreType.DMA((stop - first + 1,)),
                ],
                alias={n - 2: 0, n - 1: 1} if outs else {}, hbm=(n - 2, n - 1) if outs else (), flops=10_000_000,
            )
        if i < len(steps):
            history = jnp.maximum(history, arrived)
    return outs[0], outs[1], history


def solution(mesh):
    field = P(None, None, "gx", Y)
    layered = P(None, "gx", Y)
    plane = P("gx", Y)
    return jax.shard_map(
        on_device,
        mesh=mesh,
        in_specs=(field, field, layered, layered, field, field, layered, plane, plane),
        out_specs=(field, field, P()),
        check_vma=False,
    )
```

```python
import functools

import jax
import jax.numpy as jnp
import numpy as np
from jax import lax
from jax.experimental import pallas as pl
from jax.experimental.pallas import tpu as pltpu
from jax.sharding import PartitionSpec as P

STEPS = 2
LANES = 128
TWELFTH = 1.0 / 12.0
Y = ("grid", "gy")
ALL = ("grid", "gx", "gy")
VMEM_LIMIT = 16 << 20


def turn(x, by, axis):
    return pltpu.roll(x, by % x.shape[axis], axis)


def bands(length, copies):
    one = sum(w * np.eye(length, k=o) for o, w in ((1, 16.0), (-1, 16.0), (2, -1.0), (-2, -1.0)))
    return np.kron(np.eye(copies), one)


def lateral_tables(rows, cols):
    stack = 256 // rows
    left, right = bands(rows, stack), bands(cols, 1)
    return (
        jnp.asarray(np.concatenate([left, left], axis=1), jnp.bfloat16),
        jnp.asarray(np.concatenate([right, right], axis=0), jnp.bfloat16),
    )


def lateral12(planes, left, right):
    a = planes.astype(jnp.bfloat16)
    b = (planes - a.astype(jnp.float32)).astype(jnp.bfloat16)
    y = jnp.dot(jnp.concatenate([a, b], axis=1), right[...], preferred_element_type=jnp.float32)
    x = jnp.dot(left[...], jnp.concatenate([a, b], axis=0), preferred_element_type=jnp.float32)
    return (x + y) - 60.0 * planes


def depth12(ref, c, k):
    last = ref.shape[1] - 1

    def pair(offset):
        taps = [ref[c, k + o] for o in (-offset, offset) if not isinstance(k, int) or 0 <= k + o <= last]
        return taps[0] + taps[1] if len(taps) == 2 else taps[0]

    return 16.0 * pair(1) - pair(2) - 30.0 * ref[c, k]


def slot(p):
    return (p // 32) * LANES + (p % 32) * 4


def column_tables(planes):
    pack, unpack = np.zeros((2 * LANES, 2 * LANES)), np.zeros((2 * LANES, 2 * LANES))
    for p in range(planes):
        v0, v1, u0, u1 = (slot(p) + i for i in range(4))
        down, up = 2 * p, LANES + 2 * p
        pack[u0, down] = -1.0
        pack[u0, down + 1], pack[u1, down + 1] = 16.0, -1.0
        pack[v0, up], pack[v1, up] = -1.0, 16.0
        pack[v1, up + 1] = -1.0
        unpack[2 * p, slot(p) + 2] = unpack[2 * p + 1, slot(p) + 3] = 1.0
        unpack[LANES + 2 * p, slot(p)] = unpack[LANES + 2 * p + 1, slot(p) + 1] = 1.0
    return tuple(jnp.asarray(np.tile(t, (3, 1)), jnp.bfloat16) for t in (pack, unpack))


def pieces(x):
    a = x.astype(jnp.bfloat16)
    rest = x - a.astype(jnp.float32)
    b = rest.astype(jnp.bfloat16)
    c = (rest - b.astype(jnp.float32)).astype(jnp.bfloat16)
    return jnp.concatenate([a, b, c], axis=-1)


def times(x, table):
    return jnp.dot(pieces(x), table[...], preferred_element_type=jnp.float32)


def pack_all(uf, uc, pack, x_down, x_up, y_down, y_up, ready=None, ready_table=None):
    comps, layers, rows, cols = uf.shape
    crows, ccols = uc.shape[2:]
    raw = []
    for ref, at in ((uf, slice(0, cols)), (uc, slice(cols, cols + ccols))):
        n, width = ref.shape[2:]
        lane = lax.broadcasted_iota(jnp.int32, (n, LANES), 1)
        sub = lax.broadcasted_iota(jnp.int32, (8, width), 0)
        columns = [jnp.zeros((n, LANES), jnp.float32) for _ in range(2)]
        for g in range(0, layers, 4):
            if ready is not None:
                ready(ref is uc, g)
            for c in range(comps):
                first = last = jnp.zeros((8, width), jnp.float32)
                for i in range(4):
                    p = c * layers + g + i
                    u = ref[c, g + i, :, 0:LANES]
                    if width > LANES:
                        u = jnp.where(lane < 2, u, ref[c, g + i, :, width - LANES : width])
                    u = turn(u, slot(p) % LANES + 2, 1)
                    half = slot(p) // LANES
                    columns[half] = jnp.where(lane // 4 == slot(p) % LANES // 4, u, columns[half])
                    first = jnp.where(sub // 2 == i, turn(ref[c, g + i, 0:8, :], 2 * i, 0), first)
                    last = jnp.where(sub // 2 == i, turn(ref[c, g + i, n - 8 : n, :], 2 * i + 2, 0), last)
                tile = (c * layers + g) // 4
                x_down[tile, :, at] = jnp.where(lax.rem(sub, 2) == 1, 16.0 * turn(first, 1, 0), 0.0) - first
                x_up[tile, :, at] = jnp.where(lax.rem(sub, 2) == 0, 16.0 * turn(last, -1, 0), 0.0) - last
        raw.append(jnp.concatenate(columns, axis=1))
    if ready_table is not None:
        ready_table()
    packed = times(jnp.concatenate(raw, axis=0), pack)
    y_down[...] = packed[:, 0:LANES]
    y_up[...] = packed[:, LANES : 2 * LANES]


def load_kernel(uf_hbm, uc_hbm, pack_hbm, uf, uc, x_down, x_up, y_down, y_up, pack, sem):
    layers = uf.shape[1]
    copies = {}
    for coarse, src, dst in ((False, uf_hbm, uf), (True, uc_hbm, uc)):
        for g in range(0, layers, 4):
            at = pl.ds(g, 4)
            copies[coarse, g] = pltpu.make_async_copy(src.at[:, at], dst.at[:, at], sem.at[int(coarse), g // 4])
            copies[coarse, g].start()
    table = pltpu.make_async_copy(pack_hbm, pack, sem.at[2, 0])
    table.start()

    def ready(coarse, g):
        copies[coarse, g].wait()

    pack_all(uf, uc, pack, x_down, x_up, y_down, y_up, ready, table.wait)


def groups_do(total, size, body):
    body(0)
    if total > 2 * size:

        @pl.loop(1, total // size - 1)
        def _(g):
            body(g * size)

    body(total - size)


def main_kernel(first_step, uf, sp, me, uc, cs, tr, left_f, right_f, left_c, right_c, widen, narrow, *refs):
    comps, layers, rows, cols = uf.shape
    crows, ccols = uc.shape[2:]
    size_f, size_c = 256 // rows, 256 // crows
    if first_step:
        vf, vc, *prep, lat, tall = refs
    else:
        pf, pc, vf, vc, *prep, lat, tall = refs
    lat_c0 = prep[-1]

    def coarse(first):
        for c in range(comps):
            planes = uc[c, pl.ds(first, size_c)].reshape(256, ccols)
            part = lateral12(planes, left_c, right_c)
            if isinstance(first, int) and first == 0:
                lat_c0[c] = part[0:crows, :]
            for i in range(size_c):
                k = first + i
                old = 2.0 * uc[c, k] if first_step else 2.0 * uc[c, k] - pc[c, k]
                vc[c, k] = old + cs[k] * TWELFTH * (part[i * crows : (i + 1) * crows, :] + depth12(uc, c, k))

    def fine(first):
        for c in range(comps):
            planes = uf[c, pl.ds(first, size_f)].reshape(256, cols)
            lat[c] = lateral12(planes, left_f, right_f)
        for i in range(size_f):
            k = first + i
            s12, m2 = sp[k] * TWELFTH, me[k] * me[k]
            for c in range(comps):
                old = 2.0 * uf[c, k] if first_step else 2.0 * uf[c, k] - pf[c, k]
                vf[c, k] = old + s12 * (lat[c, i * rows : (i + 1) * rows, :] + m2 * depth12(uf, c, k))

    groups_do(layers, size_c, coarse)
    groups_do(layers, size_f, fine)
    prepare(uf, sp, me, uc, cs, tr, widen, narrow, lat, tall, *prep)


class Edges:
    def __init__(self, got, slots, shapes, unpack=None):
        self.got_xd, self.got_xu, got_yd, got_yu = got
        self.slots = slots
        (self.layers, rows, cols), (crows, ccols) = shapes
        self.fine = (slice(0, rows), slice(0, cols), rows, cols)
        self.coarse = (slice(rows, rows + crows), slice(cols, cols + ccols), crows, ccols)
        x_at, x_n = lax.axis_index("gx"), lax.axis_size("gx")
        y_at, y_n = lax.axis_index(Y), lax.axis_size(Y)
        self.x_low, self.x_high = x_at > 0, x_at < x_n - 1
        if unpack is None:
            return
        up = jnp.where(y_at > 0, got_yu[...], 0.0)
        down = jnp.where(y_at < y_n - 1, got_yd[...], 0.0)
        both = times(jnp.concatenate([up, down], axis=1), unpack)
        slots[0] = both[:, 0:LANES]
        slots[1] = both[:, LANES : 2 * LANES]

    def plane(self, grid, c, g, i):
        ys, xs, n, width = grid
        p = c * self.layers + g + i
        lane = lax.broadcasted_iota(jnp.int32, (n, LANES), 1)
        sub = lax.broadcasted_iota(jnp.int32, (8, width), 0)
        half, quad = (p // 32, p % 32) if isinstance(p, int) else (lax.div(p, 32), lax.rem(p, 32))
        u = pltpu.roll(self.slots[half, ys, :], LANES - 2 - 4 * quad, 1)
        low, high = jnp.where(lane < 2, u, 0.0), jnp.where(lane >= LANES - 2, u, 0.0)
        if width == LANES:
            columns = low + high
        else:
            columns = jnp.concatenate([low, high], axis=1)
        tile = p // 4 if isinstance(p, int) else lax.div(c * self.layers + g, 4)
        first = jnp.where(jnp.logical_and(sub < 2, self.x_low), turn(self.got_xu[tile, :, xs], -2 * i, 0), 0.0)
        last = jnp.where(jnp.logical_and(sub >= 6, self.x_high), turn(self.got_xd[tile, :, xs], 6 - 2 * i, 0), 0.0)
        return jnp.concatenate([columns[0:8] + first, columns[8 : n - 8], columns[n - 8 : n] + last], axis=0)


def stretch(planes, widen, tall, rows, cols):
    wide = times(jnp.concatenate(planes, axis=0), widen)
    n = len(planes) * rows // 2
    halves = range(cols // LANES)
    for half in halves:
        part = wide[:, half * LANES : (half + 1) * LANES]
        tall[half, pl.ds(0, n, 2), :] = part
        tall[half, pl.ds(1, n, 2), :] = part
    return [
        jnp.concatenate([tall[half, i * rows : (i + 1) * rows, :] for half in halves], axis=1)
        for i in range(len(planes))
    ]


def row_pairs(planes, tall):
    rows, cols = planes[0].shape
    n = len(planes) * rows // 2
    halves = range(cols // LANES)
    for i, plane in enumerate(planes):
        for half in halves:
            tall[half, i * rows : (i + 1) * rows, :] = plane[:, half * LANES : (half + 1) * LANES]
    return tuple(
        jnp.concatenate([tall[half, pl.ds(start, n, 2), :] for half in halves], axis=1) for start in range(2)
    )


def prepare(uf, sp, me, uc, cs, tr, widen, narrow, lat, tall, alpha_o, gain_o, metric_o, beta_o, first_o, sums_o, top_o, lat_c0):
    comps, layers, rows, cols = uf.shape
    b = layers - 1
    s, m = sp[b], me[b]
    m2 = m * m
    gain = 1.0 / (s * m2)
    inv_m2 = 1.0 / m2
    cs0 = cs[0]
    t = tr[...]
    c0 = [uc[c, 0] for c in range(comps)]
    pull = [
        cs0 * (lat_c0[c] - 29.0 * uc[c, 0] + 16.0 * uc[c, 1] - uc[c, 2]) * TWELFTH for c in range(comps)
    ]
    wide = stretch([cs0] + pull + c0, widen, tall, rows, cols)
    alpha = gain * wide[0]
    gain14 = gain * (12.0 / 14.0)
    alpha_o[...] = alpha
    gain_o[...] = gain14
    metric_o[...] = inv_m2 * (1.0 / 14.0)
    weighted = []
    for c in range(comps):
        ub, u1, u2 = uf[c, b], uf[c, b - 1], uf[c, b - 2]
        e = u2 - lat[c, 256 - rows : 256, :] * inv_m2 - 16.0 * u1 + 29.0 * ub
        bc = gain14 * wide[1 + c] + e * (1.0 / 14.0)
        beta_o[c] = bc
        first_o[c] = alpha * wide[1 + comps + c] - ub
        weighted.append(t * bc)
        weighted.append(t * (u2 - 8.0 * u1 + 7.0 * ub))
        weighted.append(t * (u2 - 8.0 * u1 + ub))
    even_rows, odd_rows = row_pairs([t * alpha] + weighted, tall)
    sums_o[...] = times(even_rows + odd_rows, narrow)
    even_rows, odd_rows = row_pairs([alpha], tall)
    top = jnp.maximum(even_rows, odd_rows)
    top = jnp.maximum(top, turn(top, -1, 1))
    lane = lax.broadcasted_iota(jnp.int32, top.shape, 1)
    top_o[...] = times(jnp.where(lax.rem(lane, 2) == 0, top, 0.0), narrow)


def interface(edges, uc, cs, tr, sh, widen, narrow, tall, alpha, gain14, metric14, beta_in, first_in, sums, top, lat_c0):
    comps, rows, cols = beta_in.shape
    crows, ccols = sh.shape
    layers = edges.layers
    inv_sh = 1.0 / sh[...]
    t = tr[...]
    pull = [cs[0] * TWELFTH * edges.plane(edges.coarse, c, 0, 0) for c in range(comps)]
    wide = stretch(pull, widen, tall, rows, cols)
    beta, weighted, first = [], [], None
    for c in range(comps):
        more = gain14[...] * wide[c] - metric14[...] * edges.plane(edges.fine, c, layers - 4, 3)
        bc = beta_in[c] + more
        beta.append(bc)
        weighted.append(t * more)
        change = jnp.max(jnp.abs(first_in[c] + bc), axis=0, keepdims=True)
        first = change if first is None else jnp.maximum(first, change)
    even_rows, odd_rows = row_pairs(weighted, tall)
    more = times(even_rows + odd_rows, narrow)

    def part(i):
        return sums[i * crows : (i + 1) * crows, :]

    rate = part(0) * (0.5 * inv_sh)
    history = [[], [], [], []]
    c3s, c4s = [], []
    for c in range(comps):
        c0 = uc[c, 0]
        q6 = (8.0 * uc[c, 1] - c0 - uc[c, 2]) * (1.0 / 6.0)
        pushed = part(1 + 3 * c) + more[c * crows : (c + 1) * crows, :]
        start, still = part(2 + 3 * c), part(3 + 3 * c)
        base = q6 - (still * TWELFTH + 0.5 * pushed) * inv_sh
        c1 = q6 - start * (TWELFTH * inv_sh)
        c2 = base - rate * c0
        c3 = base - rate * c1
        c4 = base - rate * c2
        d1, d2, d3, d4 = (jnp.abs(x) for x in (c1 - c0, c2 - c1, c3 - c2, c4 - c3))
        history[0].append(d1)
        history[1].append(jnp.maximum(d2, top[...] * d1))
        history[2].append(jnp.maximum(d3, top[...] * d2))
        history[3].append(jnp.maximum(d4, top[...] * d3))
        c3s.append(c3)
        c4s.append(c4)
    lane = lax.broadcasted_iota(jnp.int32, (1, LANES), 1)
    line = jnp.zeros((1, LANES), jnp.float32)
    for n in range(4):
        d = jnp.maximum(jnp.maximum(history[n][0], history[n][1]), history[n][2])
        d = jnp.max(d, axis=0, keepdims=True)
        if n == 0:
            for half in range(cols // LANES):
                d = jnp.maximum(d, first[:, half * LANES : (half + 1) * LANES])
        line = jnp.where(lane == n, jnp.max(d, axis=1, keepdims=True), line)
    wide = stretch(c3s, widen, tall, rows, cols)
    return [alpha[...] * wide[c] + beta[c] for c in range(comps)], c4s, line[:, 0:4]


PREP = 8


def fix_kernel(vf_in, vc_in, pack, unpack, uf, pf, sp, me, uc, pc, cs, tr, sh, widen, narrow, *refs):
    prep, got = refs[:PREP], refs[PREP : PREP + 4]
    vf, vc, change, *packed = refs[PREP + 4 : -2]
    tall, slots = refs[-2:]
    comps, layers, rows, cols = uf.shape
    edges = Edges(got, slots, (uf.shape[1:], uc.shape[2:]), unpack)
    ghost_f, ghost_c, line = interface(edges, uc, cs, tr, sh, widen, narrow, tall, *prep)
    change[...] = line
    b = layers - 1
    s_last = sp[b] * me[b] * me[b] * TWELFTH
    s_next = sp[b - 1] * me[b - 1] * me[b - 1] * TWELFTH
    for c in range(comps):
        vf[c, b] = vf_in[c, b] + s_last * (14.0 * ghost_f[c] + uf[c, b])
        vf[c, b - 1] = vf_in[c, b - 1] - s_next * ghost_f[c]
        vc[c, 0] = vc_in[c, 0] + cs[0] * TWELFTH * (14.0 * ghost_c[c] + uc[c, 0])
        vc[c, 1] = vc_in[c, 1] - cs[1] * TWELFTH * ghost_c[c]

    @pl.loop(0, layers // 4)
    def _(quarter):
        g = quarter * 4
        for i in range(4):
            s12, cs12 = sp[g + i] * TWELFTH, cs[g + i] * TWELFTH
            for c in range(comps):
                vf[c, g + i] = vf_in[c, g + i] - pf[c, g + i] + s12 * edges.plane(edges.fine, c, g, i)
                vc[c, g + i] = vc_in[c, g + i] - pc[c, g + i] + cs12 * edges.plane(edges.coarse, c, g, i)

    pack_all(vf, vc, pack, *packed)


def interface_kernel(unpack, uf, uc, cs, tr, sh, widen, narrow, *refs):
    prep, got = refs[:PREP], refs[PREP : PREP + 4]
    ghost_f, ghost_c, change, slots, tall = refs[PREP + 4 :]
    edges = Edges(got, slots, (uf.shape[1:], uc.shape[2:]), unpack)
    g, c4, line = interface(edges, uc, cs, tr, sh, widen, narrow, tall, *prep)
    for c in range(uf.shape[0]):
        ghost_f[c] = g[c]
        ghost_c[c] = c4[c]
    change[...] = line


def last_kernel(change0, change1, sp, me, cs, uf, uc, vf, vc, ghost_f, ghost_c, slots, *refs):
    got = refs[0:4]
    out_f, out_c, spread, done_f, done_c, sem = refs[4:]
    comps, layers, rows, cols = uf.shape
    b = layers - 1
    edges = Edges(got, slots, (uf.shape[1:], uc.shape[2:]))
    for step, line in enumerate((change0, change1)):
        spread[:, step : step + 1, :] = jnp.broadcast_to(line[...][None], (spread.shape[0], 1, spread.shape[2]))

    def copy(k):
        return pltpu.make_async_copy(done_f.at[:, k], out_f.at[:, k], sem.at[k])

    copy_coarse = pltpu.make_async_copy(done_c, out_c, sem.at[layers])

    def fine(k, g, i):
        s12 = sp[k] * TWELFTH
        for c in range(comps):
            total = edges.plane(edges.fine, c, g, i)
            if isinstance(k, int) and k == b:
                total = total + me[k] * me[k] * (14.0 * ghost_f[c] + uf[c, b])
            if isinstance(k, int) and k == b - 1:
                total = total - me[k] * me[k] * ghost_f[c]
            done_f[c, k] = vf[c, k] + s12 * total
        copy(k).start()

    @pl.loop(0, layers // 4 - 1)
    def _(quarter):
        for i in range(4):
            fine(quarter * 4 + i, quarter * 4, i)

    for i in range(4):
        fine(layers - 4 + i, layers - 4, i)

    @pl.loop(0, layers // 4)
    def _(quarter):
        g = quarter * 4
        for i in range(4):
            cs12 = cs[g + i] * TWELFTH
            for c in range(comps):
                done_c[c, g + i] = vc[c, g + i] + cs12 * edges.plane(edges.coarse, c, g, i)

    for c in range(comps):
        done_c[c, 0] = done_c[c, 0] + cs[0] * TWELFTH * (14.0 * ghost_c[c] + uc[c, 0])
        done_c[c, 1] = done_c[c, 1] - cs[1] * TWELFTH * ghost_c[c]
    copy_coarse.start()
    for k in range(layers):
        copy(k).wait()
    copy_coarse.wait()


def call(kernel, args, outs, scratch=(), alias={}, flops=0, hbm=()):
    spaces = [pltpu.HBM if i in hbm else pltpu.VMEM for i in range(len(args))]
    return pl.pallas_call(
        kernel,
        out_shape=tuple(outs),
        in_specs=[pl.BlockSpec(memory_space=s) for s in spaces],
        out_specs=tuple(pl.BlockSpec(memory_space=o.memory_space) for o in outs),
        scratch_shapes=list(scratch),
        input_output_aliases=alias,
        cost_estimate=pl.CostEstimate(flops=flops, bytes_accessed=flops, transcendentals=0),
        compiler_params=pltpu.CompilerParams(vmem_limit_bytes=VMEM_LIMIT),
    )(*[pltpu.with_memory_space_constraint(x, s) for x, s in zip(args, spaces)])


def exchange(parts):
    x_down, x_up, y_down, y_up = parts

    def ring(value, axis, by):
        n = lax.axis_size(axis)
        return lax.ppermute(value, axis, [(i, (i + by) % n) for i in range(n)])

    return (ring(x_down, "gx", -1), ring(x_up, "gx", 1), ring(y_down, Y, -1), ring(y_up, Y, 1))


def on_device(
    fine_field, fine_previous, fine_speed, fine_metric, coarse_field, coarse_previous, coarse_speed,
    fine_traction, coarse_shear,
):
    f32 = jnp.float32
    comps, layers, rows, cols = fine_field.shape
    crows, ccols = coarse_field.shape[2:]
    fine = pltpu.VMEM(fine_field.shape, f32)
    coarse = pltpu.VMEM(coarse_field.shape, f32)
    plane_f = pltpu.VMEM((comps, rows, cols), f32)
    plane_c = pltpu.VMEM((comps, crows, ccols), f32)
    line = pltpu.VMEM((1, 4), f32)
    corrections = pltpu.VMEM((2, rows + crows, LANES), f32)
    edge_outs = [
        pltpu.VMEM((comps * layers // 4, 8, cols + ccols), f32),
        pltpu.VMEM((comps * layers // 4, 8, cols + ccols), f32),
        pltpu.VMEM((rows + crows, LANES), f32),
        pltpu.VMEM((rows + crows, LANES), f32),
    ]
    tall = pltpu.VMEM((cols // LANES, 10 * rows, LANES), f32)
    prep_outs = [pltpu.VMEM((rows, cols), f32)] * 3 + [plane_f, plane_f]
    prep_outs += [pltpu.VMEM((10 * crows, ccols), f32), pltpu.VMEM((crows, ccols), f32), plane_c]
    picks = np.zeros((cols, ccols), np.float32)
    picks[np.arange(cols), np.arange(cols) // 2] = 1.0
    narrow = jnp.asarray(np.tile(picks, (3, 1)), jnp.bfloat16)
    widen = jnp.asarray(np.tile(picks.T, (3, 1)), jnp.bfloat16)
    tables = (*lateral_tables(rows, cols), *lateral_tables(crows, ccols), widen, narrow)
    pack, unpack = column_tables(comps * layers)
    lat = pltpu.VMEM((comps, 256, cols), f32)
    tr, sh = fine_traction, coarse_shear

    uf, uc, *mine = call(
        load_kernel, (fine_field, coarse_field, pack), [fine, coarse] + edge_outs,
        scratch=[pltpu.VMEM(pack.shape, pack.dtype), pltpu.SemaphoreType.DMA((3, layers // 4))], hbm=(0, 1, 2),
    )
    theirs = exchange(mine)
    sp, me, cs = fine_speed, fine_metric, coarse_speed
    vf, vc, *prep = call(
        functools.partial(main_kernel, True), (uf, sp, me, uc, cs, tr, *tables), [fine, coarse, *prep_outs],
        scratch=[lat, tall], flops=40_000_000,
    )
    vf, vc, change0, *mine = call(
        fix_kernel,
        (vf, vc, pack, unpack, uf, fine_previous, sp, me, uc, coarse_previous, cs, tr, sh, widen, narrow, *prep, *theirs),
        [fine, coarse, line] + edge_outs, scratch=[tall, corrections], alias={0: 0, 1: 1}, flops=20_000_000,
    )
    pf, pc, uf, uc = uf, uc, vf, vc
    theirs = exchange(mine)
    vf, vc, *prep = call(
        functools.partial(main_kernel, False), (uf, sp, me, uc, cs, tr, *tables, pf, pc), [fine, coarse, *prep_outs],
        scratch=[lat, tall], flops=40_000_000,
    )
    ghost_f, ghost_c, change1, slots = call(
        interface_kernel, (unpack, uf, uc, cs, tr, sh, widen, narrow, *prep, *theirs),
        [plane_f, plane_c, line, corrections], scratch=[tall], flops=10_000_000,
    )
    n = lax.axis_size(ALL)
    out_f, out_c, spread = call(
        last_kernel,
        (change0, change1, sp, me, cs, uf, uc, vf, vc, ghost_f, ghost_c, slots, *theirs),
        [pltpu.HBM(fine_field.shape, f32), pltpu.HBM(coarse_field.shape, f32), pltpu.VMEM((n, STEPS, 4), f32)],
        scratch=[fine, coarse, pltpu.SemaphoreType.DMA((layers + 1,))], flops=40_000_000,
    )
    return out_f, out_c, jnp.max(lax.all_to_all(spread, ALL, 0, 0, tiled=True), axis=0)


def solution(mesh):
    field = P(None, None, "gx", Y)
    layered = P(None, "gx", Y)
    plane = P("gx", Y)
    return jax.shard_map(
        on_device,
        mesh=mesh,
        in_specs=(field, field, layered, layered, field, field, layered, plane, plane),
        out_specs=(field, field, P()),
        check_vma=False,
    )
```

```python
import functools

import jax
import jax.numpy as jnp
import numpy as np
from jax import lax
from jax.experimental import pallas as pl
from jax.experimental.pallas import tpu as pltpu
from jax.sharding import PartitionSpec as P

STEPS = 2
LANES = 128
TWELFTH = 1.0 / 12.0
Y = ("grid", "gy")
ALL = ("grid", "gx", "gy")
VMEM_LIMIT = 16 << 20


def turn(x, by, axis):
    return pltpu.roll(x, by % x.shape[axis], axis)


def bands(length, copies):
    one = sum(w * np.eye(length, k=o) for o, w in ((1, 16.0), (-1, 16.0), (2, -1.0), (-2, -1.0)))
    return np.kron(np.eye(copies), one)


def lateral_tables(rows, cols):
    stack = 256 // rows
    left, right = bands(rows, stack), bands(cols, 1)
    return (
        jnp.asarray(np.concatenate([left, left], axis=1), jnp.bfloat16),
        jnp.asarray(np.concatenate([right, right], axis=0), jnp.bfloat16),
    )


def lateral12(planes, left, right):
    a = planes.astype(jnp.bfloat16)
    b = (planes - a.astype(jnp.float32)).astype(jnp.bfloat16)
    y = jnp.dot(jnp.concatenate([a, b], axis=1), right[...], preferred_element_type=jnp.float32)
    x = jnp.dot(left[...], jnp.concatenate([a, b], axis=0), preferred_element_type=jnp.float32)
    return (x + y) - 60.0 * planes


def depth12(ref, c, k):
    last = ref.shape[1] - 1

    def pair(offset):
        taps = [ref[c, k + o] for o in (-offset, offset) if not isinstance(k, int) or 0 <= k + o <= last]
        return taps[0] + taps[1] if len(taps) == 2 else taps[0]

    return 16.0 * pair(1) - pair(2) - 30.0 * ref[c, k]


def slot(p):
    return (p // 32) * LANES + (p % 32) * 4


def column_tables(planes):
    pack, unpack = np.zeros((2 * LANES, 2 * LANES)), np.zeros((2 * LANES, 2 * LANES))
    for p in range(planes):
        v0, v1, u0, u1 = (slot(p) + i for i in range(4))
        down, up = 2 * p, LANES + 2 * p
        pack[u0, down] = -1.0
        pack[u0, down + 1], pack[u1, down + 1] = 16.0, -1.0
        pack[v0, up], pack[v1, up] = -1.0, 16.0
        pack[v1, up + 1] = -1.0
        unpack[2 * p, slot(p) + 2] = unpack[2 * p + 1, slot(p) + 3] = 1.0
        unpack[LANES + 2 * p, slot(p)] = unpack[LANES + 2 * p + 1, slot(p) + 1] = 1.0
    return tuple(jnp.asarray(np.tile(t, (3, 1)), jnp.bfloat16) for t in (pack, unpack))


def pieces(x):
    a = x.astype(jnp.bfloat16)
    rest = x - a.astype(jnp.float32)
    b = rest.astype(jnp.bfloat16)
    c = (rest - b.astype(jnp.float32)).astype(jnp.bfloat16)
    return jnp.concatenate([a, b, c], axis=-1)


def times(x, table):
    return jnp.dot(pieces(x), table[...], preferred_element_type=jnp.float32)


def pack_all(uf, uc, pack, x_down, x_up, y_down, y_up, ready=None, ready_table=None):
    comps, layers, rows, cols = uf.shape
    crows, ccols = uc.shape[2:]
    raw = []
    for ref, at in ((uf, slice(0, cols)), (uc, slice(cols, cols + ccols))):
        n, width = ref.shape[2:]
        lane = lax.broadcasted_iota(jnp.int32, (n, LANES), 1)
        sub = lax.broadcasted_iota(jnp.int32, (8, width), 0)
        columns = [jnp.zeros((n, LANES), jnp.float32) for _ in range(2)]
        for g in range(0, layers, 4):
            if ready is not None:
                ready(ref is uc, g)
            for c in range(comps):
                first = last = jnp.zeros((8, width), jnp.float32)
                for i in range(4):
                    p = c * layers + g + i
                    u = ref[c, g + i, :, 0:LANES]
                    if width > LANES:
                        u = jnp.where(lane < 2, u, ref[c, g + i, :, width - LANES : width])
                    u = turn(u, slot(p) % LANES + 2, 1)
                    half = slot(p) // LANES
                    columns[half] = jnp.where(lane // 4 == slot(p) % LANES // 4, u, columns[half])
                    first = jnp.where(sub // 2 == i, turn(ref[c, g + i, 0:8, :], 2 * i, 0), first)
                    last = jnp.where(sub // 2 == i, turn(ref[c, g + i, n - 8 : n, :], 2 * i + 2, 0), last)
                tile = (c * layers + g) // 4
                x_down[tile, :, at] = jnp.where(lax.rem(sub, 2) == 1, 16.0 * turn(first, 1, 0), 0.0) - first
                x_up[tile, :, at] = jnp.where(lax.rem(sub, 2) == 0, 16.0 * turn(last, -1, 0), 0.0) - last
        raw.append(jnp.concatenate(columns, axis=1))
    if ready_table is not None:
        ready_table()
    packed = times(jnp.concatenate(raw, axis=0), pack)
    y_down[...] = packed[:, 0:LANES]
    y_up[...] = packed[:, LANES : 2 * LANES]


def load_kernel(uf_hbm, uc_hbm, pack_hbm, uf, uc, x_down, x_up, y_down, y_up, pack, sem):
    layers = uf.shape[1]
    copies = {}
    for coarse, src, dst in ((False, uf_hbm, uf), (True, uc_hbm, uc)):
        for g in range(0, layers, 4):
            at = pl.ds(g, 4)
            copies[coarse, g] = pltpu.make_async_copy(src.at[:, at], dst.at[:, at], sem.at[int(coarse), g // 4])
            copies[coarse, g].start()
    table = pltpu.make_async_copy(pack_hbm, pack, sem.at[2, 0])
    table.start()

    def ready(coarse, g):
        copies[coarse, g].wait()

    pack_all(uf, uc, pack, x_down, x_up, y_down, y_up, ready, table.wait)


def main_kernel(first_step, uf, sp, me, uc, cs, tr, left_f, right_f, left_c, right_c, widen, narrow, *refs):
    comps, layers, rows, cols = uf.shape
    crows, ccols = uc.shape[2:]
    size_f, size_c = 256 // rows, 256 // crows
    if first_step:
        vf, vc, *fixed, beta, first, sums, lat_c0, lat, tall = refs
    else:
        *fixed, pf, pc, vf, vc, beta, first, sums, lat_c0, lat, tall = refs

    def coarse(start):
        for c in range(comps):
            planes = uc[c, start : start + size_c].reshape(256, ccols)
            part = lateral12(planes, left_c, right_c)
            if start == 0:
                lat_c0[c] = part[0:crows, :]
            for i in range(size_c):
                k = start + i
                old = 2.0 * uc[c, k] if first_step else 2.0 * uc[c, k] - pc[c, k]
                vc[c, k] = old + cs[k] * TWELFTH * (part[i * crows : (i + 1) * crows, :] + depth12(uc, c, k))

    def fine_lateral(start):
        for c in range(comps):
            planes = uf[c, start : start + size_f].reshape(256, cols)
            lat[start // size_f % 2, c] = lateral12(planes, left_f, right_f)

    def fine(start):
        for i in range(size_f):
            k = start + i
            s12, m2 = sp[k] * TWELFTH, me[k] * me[k]
            for c in range(comps):
                old = 2.0 * uf[c, k] if first_step else 2.0 * uf[c, k] - pf[c, k]
                side = lat[start // size_f % 2, c, i * rows : (i + 1) * rows, :]
                vf[c, k] = old + s12 * (side + m2 * depth12(uf, c, k))

    fine_lateral(0)
    for start in range(0, layers, size_f):
        if start + size_f < layers:
            fine_lateral(start + size_f)
        fine(start)
    if first_step:
        prepare_fixed(sp, me, cs, tr, widen, narrow, tall, *fixed)
    lat_b = lat.at[(layers - 1) // size_f % 2, :, 256 - rows : 256]
    for start in range(0, layers, size_c):
        coarse(start)
    prepare(uf, uc, cs, tr, widen, narrow, lat_b, tall, *fixed, beta, first, sums, lat_c0)


class Edges:
    def __init__(self, got, slots, shapes, unpack=None):
        self.got_xd, self.got_xu, got_yd, got_yu = got
        self.slots = slots
        (self.layers, rows, cols), (crows, ccols) = shapes
        self.fine = (slice(0, rows), slice(0, cols), rows, cols)
        self.coarse = (slice(rows, rows + crows), slice(cols, cols + ccols), crows, ccols)
        x_at, x_n = lax.axis_index("gx"), lax.axis_size("gx")
        y_at, y_n = lax.axis_index(Y), lax.axis_size(Y)
        self.x_low, self.x_high = x_at > 0, x_at < x_n - 1
        if unpack is None:
            return
        up = jnp.where(y_at > 0, got_yu[...], 0.0)
        down = jnp.where(y_at < y_n - 1, got_yd[...], 0.0)
        both = times(jnp.concatenate([up, down], axis=1), unpack)
        slots[0] = both[:, 0:LANES]
        slots[1] = both[:, LANES : 2 * LANES]

    def plane(self, grid, c, g, i):
        ys, xs, n, width = grid
        p = c * self.layers + g + i
        lane = lax.broadcasted_iota(jnp.int32, (n, LANES), 1)
        sub = lax.broadcasted_iota(jnp.int32, (8, width), 0)
        half, quad = (p // 32, p % 32) if isinstance(p, int) else (lax.div(p, 32), lax.rem(p, 32))
        u = pltpu.roll(self.slots[half, ys, :], LANES - 2 - 4 * quad, 1)
        low, high = jnp.where(lane < 2, u, 0.0), jnp.where(lane >= LANES - 2, u, 0.0)
        if width == LANES:
            columns = low + high
        else:
            columns = jnp.concatenate([low, high], axis=1)
        tile = p // 4 if isinstance(p, int) else lax.div(c * self.layers + g, 4)
        first = jnp.where(jnp.logical_and(sub < 2, self.x_low), turn(self.got_xu[tile, :, xs], -2 * i, 0), 0.0)
        last = jnp.where(jnp.logical_and(sub >= 6, self.x_high), turn(self.got_xd[tile, :, xs], 6 - 2 * i, 0), 0.0)
        return jnp.concatenate([columns[0:8] + first, columns[8 : n - 8], columns[n - 8 : n] + last], axis=0)


def stretch(planes, widen, tall, rows, cols):
    wide = times(jnp.concatenate(planes, axis=0), widen)
    n = len(planes) * rows // 2
    halves = range(cols // LANES)
    for half in halves:
        part = wide[:, half * LANES : (half + 1) * LANES]
        tall[half, pl.ds(0, n, 2), :] = part
        tall[half, pl.ds(1, n, 2), :] = part
    return [
        jnp.concatenate([tall[half, i * rows : (i + 1) * rows, :] for half in halves], axis=1)
        for i in range(len(planes))
    ]


def row_pairs(planes, tall):
    rows, cols = planes[0].shape
    n = len(planes) * rows // 2
    halves = range(cols // LANES)
    for i, plane in enumerate(planes):
        for half in halves:
            tall[half, i * rows : (i + 1) * rows, :] = plane[:, half * LANES : (half + 1) * LANES]
    return tuple(
        jnp.concatenate([tall[half, pl.ds(start, n, 2), :] for half in halves], axis=1) for start in range(2)
    )


def prepare_fixed(sp, me, cs, tr, widen, narrow, tall, alpha_o, gain_o, metric_o, rate_o, top_o):
    rows, cols = tr.shape
    b = sp.shape[0] - 1
    s, m = sp[b], me[b]
    m2 = m * m
    gain = 1.0 / (s * m2)
    alpha = gain * stretch([cs[0]], widen, tall, rows, cols)[0]
    alpha_o[...] = alpha
    gain_o[...] = gain * (12.0 / 14.0)
    metric_o[...] = (1.0 / 14.0) / m2
    even_rows, odd_rows = row_pairs([tr[...] * alpha, alpha], tall)
    crows = rows // 2
    top = jnp.maximum(even_rows[crows:], odd_rows[crows:])
    top = jnp.maximum(top, turn(top, -1, 1))
    lane = lax.broadcasted_iota(jnp.int32, top.shape, 1)
    top = jnp.where(lax.rem(lane, 2) == 0, top, 0.0)
    both = times(jnp.concatenate([even_rows[:crows] + odd_rows[:crows], top], axis=0), narrow)
    rate_o[...] = both[:crows]
    top_o[...] = both[crows:]


def prepare(uf, uc, cs, tr, widen, narrow, lat_b, tall, alpha, gain14, metric14, rate, top, beta_o, first_o, sums_o, lat_c0):
    comps, layers, rows, cols = uf.shape
    b = layers - 1
    t = tr[...]
    c0 = [uc[c, 0] for c in range(comps)]
    pull = [
        cs[0] * (lat_c0[c] - 29.0 * uc[c, 0] + 16.0 * uc[c, 1] - uc[c, 2]) * TWELFTH for c in range(comps)
    ]
    wide = stretch(pull + c0, widen, tall, rows, cols)
    weighted = []
    for c in range(comps):
        ub, u1, u2 = uf[c, b], uf[c, b - 1], uf[c, b - 2]
        bc = gain14[...] * wide[c] - metric14[...] * lat_b[c] + (u2 - 16.0 * u1 + 29.0 * ub) * (1.0 / 14.0)
        beta_o[c] = bc
        first_o[c] = alpha[...] * wide[comps + c] - ub
        still = (u2 - 8.0 * u1 + ub) * TWELFTH
        weighted.append(t * (still + 0.5 * bc))
        weighted.append(t * (still + 0.5 * ub))
    even_rows, odd_rows = row_pairs(weighted, tall)
    sums_o[...] = times(even_rows + odd_rows, narrow)


def interface(edges, uc, cs, tr, sh, widen, narrow, tall, alpha, gain14, metric14, rate_in, top, beta_in, first_in, sums):
    comps, rows, cols = beta_in.shape
    crows, ccols = sh.shape
    layers = edges.layers
    inv_sh = 1.0 / sh[...]
    t = tr[...]
    pull = [cs[0] * TWELFTH * edges.plane(edges.coarse, c, 0, 0) for c in range(comps)]
    wide = stretch(pull, widen, tall, rows, cols)
    beta, weighted, first = [], [], None
    for c in range(comps):
        more = gain14[...] * wide[c] - metric14[...] * edges.plane(edges.fine, c, layers - 4, 3)
        bc = beta_in[c] + more
        beta.append(bc)
        weighted.append(0.5 * t * more)
        change = jnp.max(jnp.abs(first_in[c] + bc), axis=0, keepdims=True)
        first = change if first is None else jnp.maximum(first, change)
    even_rows, odd_rows = row_pairs(weighted, tall)
    more = times(even_rows + odd_rows, narrow)

    def part(i):
        return sums[i * crows : (i + 1) * crows, :]

    rate = rate_in[...] * (0.5 * inv_sh)
    history = [[], [], [], []]
    c3s, c4s = [], []
    for c in range(comps):
        c0 = uc[c, 0]
        q6 = (8.0 * uc[c, 1] - c0 - uc[c, 2]) * (1.0 / 6.0)
        base = q6 - (part(2 * c) + more[c * crows : (c + 1) * crows, :]) * inv_sh
        c1 = q6 - part(2 * c + 1) * inv_sh
        c2 = base - rate * c0
        c3 = base - rate * c1
        c4 = base - rate * c2
        d1, d2, d3, d4 = (jnp.abs(x) for x in (c1 - c0, c2 - c1, c3 - c2, c4 - c3))
        history[0].append(d1)
        history[1].append(jnp.maximum(d2, top[...] * d1))
        history[2].append(jnp.maximum(d3, top[...] * d2))
        history[3].append(jnp.maximum(d4, top[...] * d3))
        c3s.append(c3)
        c4s.append(c4)
    lane = lax.broadcasted_iota(jnp.int32, (1, LANES), 1)
    line = jnp.zeros((1, LANES), jnp.float32)
    for n in range(4):
        d = jnp.maximum(jnp.maximum(history[n][0], history[n][1]), history[n][2])
        d = jnp.max(d, axis=0, keepdims=True)
        if n == 0:
            for half in range(cols // LANES):
                d = jnp.maximum(d, first[:, half * LANES : (half + 1) * LANES])
        line = jnp.where(lane == n, jnp.max(d, axis=1, keepdims=True), line)
    wide = stretch(c3s, widen, tall, rows, cols)
    return [alpha[...] * wide[c] + beta[c] for c in range(comps)], c4s, line[:, 0:4]


PREP = 8


def fix_kernel(vf_in, vc_in, pack, unpack, uf, pf, sp, me, uc, pc, cs, tr, sh, widen, narrow, *refs):
    prep, got = refs[:PREP], refs[PREP : PREP + 4]
    vf, vc, change, *packed = refs[PREP + 4 : -2]
    tall, slots = refs[-2:]
    comps, layers, rows, cols = uf.shape
    edges = Edges(got, slots, (uf.shape[1:], uc.shape[2:]), unpack)
    ghost_f, ghost_c, line = interface(edges, uc, cs, tr, sh, widen, narrow, tall, *prep)
    change[...] = line
    b = layers - 1
    s_last = sp[b] * me[b] * me[b] * TWELFTH
    s_next = sp[b - 1] * me[b - 1] * me[b - 1] * TWELFTH
    for c in range(comps):
        vf[c, b] = vf_in[c, b] + s_last * (14.0 * ghost_f[c] + uf[c, b])
        vf[c, b - 1] = vf_in[c, b - 1] - s_next * ghost_f[c]
        vc[c, 0] = vc_in[c, 0] + cs[0] * TWELFTH * (14.0 * ghost_c[c] + uc[c, 0])
        vc[c, 1] = vc_in[c, 1] - cs[1] * TWELFTH * ghost_c[c]

    for g in range(0, layers, 4):
        for i in range(4):
            s12, cs12 = sp[g + i] * TWELFTH, cs[g + i] * TWELFTH
            for c in range(comps):
                vf[c, g + i] = vf_in[c, g + i] - pf[c, g + i] + s12 * edges.plane(edges.fine, c, g, i)
                vc[c, g + i] = vc_in[c, g + i] - pc[c, g + i] + cs12 * edges.plane(edges.coarse, c, g, i)

    pack_all(vf, vc, pack, *packed)


def interface_kernel(unpack, uf, uc, cs, tr, sh, widen, narrow, *refs):
    prep, got = refs[:PREP], refs[PREP : PREP + 4]
    ghost_f, ghost_c, change, slots, tall = refs[PREP + 4 :]
    edges = Edges(got, slots, (uf.shape[1:], uc.shape[2:]), unpack)
    g, c4, line = interface(edges, uc, cs, tr, sh, widen, narrow, tall, *prep)
    for c in range(uf.shape[0]):
        ghost_f[c] = g[c]
        ghost_c[c] = c4[c]
    change[...] = line


def last_kernel(change0, change1, sp, me, cs, uf, uc, vf, vc, ghost_f, ghost_c, slots, *refs):
    got = refs[0:4]
    out_f, out_c, spread, done_f, done_c, sem = refs[4:]
    comps, layers, rows, cols = uf.shape
    b = layers - 1
    edges = Edges(got, slots, (uf.shape[1:], uc.shape[2:]))
    for step, line in enumerate((change0, change1)):
        spread[:, step : step + 1, :] = jnp.broadcast_to(line[...][None], (spread.shape[0], 1, spread.shape[2]))

    def copy(k):
        return pltpu.make_async_copy(done_f.at[:, k], out_f.at[:, k], sem.at[k])

    copy_coarse = pltpu.make_async_copy(done_c, out_c, sem.at[layers])

    def fine(k, g, i):
        s12 = sp[k] * TWELFTH
        for c in range(comps):
            total = edges.plane(edges.fine, c, g, i)
            if isinstance(k, int) and k == b:
                total = total + me[k] * me[k] * (14.0 * ghost_f[c] + uf[c, b])
            if isinstance(k, int) and k == b - 1:
                total = total - me[k] * me[k] * ghost_f[c]
            done_f[c, k] = vf[c, k] + s12 * total
        copy(k).start()

    for k in range(layers):
        fine(k, k // 4 * 4, k % 4)

    for g in range(0, layers, 4):
        for i in range(4):
            cs12 = cs[g + i] * TWELFTH
            for c in range(comps):
                done_c[c, g + i] = vc[c, g + i] + cs12 * edges.plane(edges.coarse, c, g, i)

    for c in range(comps):
        done_c[c, 0] = done_c[c, 0] + cs[0] * TWELFTH * (14.0 * ghost_c[c] + uc[c, 0])
        done_c[c, 1] = done_c[c, 1] - cs[1] * TWELFTH * ghost_c[c]
    copy_coarse.start()
    for k in range(layers):
        copy(k).wait()
    copy_coarse.wait()


def call(kernel, args, outs, scratch=(), alias={}, flops=0, hbm=()):
    spaces = [pltpu.HBM if i in hbm else pltpu.VMEM for i in range(len(args))]
    return pl.pallas_call(
        kernel,
        out_shape=tuple(outs),
        in_specs=[pl.BlockSpec(memory_space=s) for s in spaces],
        out_specs=tuple(pl.BlockSpec(memory_space=o.memory_space) for o in outs),
        scratch_shapes=list(scratch),
        input_output_aliases=alias,
        cost_estimate=pl.CostEstimate(flops=flops, bytes_accessed=flops, transcendentals=0),
        compiler_params=pltpu.CompilerParams(vmem_limit_bytes=VMEM_LIMIT),
    )(*[pltpu.with_memory_space_constraint(x, s) for x, s in zip(args, spaces)])


def exchange(parts):
    x_down, x_up, y_down, y_up = parts

    def ring(value, axis, by):
        n = lax.axis_size(axis)
        return lax.ppermute(value, axis, [(i, (i + by) % n) for i in range(n)])

    return (ring(x_down, "gx", -1), ring(x_up, "gx", 1), ring(y_down, Y, -1), ring(y_up, Y, 1))


def on_device(
    fine_field, fine_previous, fine_speed, fine_metric, coarse_field, coarse_previous, coarse_speed,
    fine_traction, coarse_shear,
):
    f32 = jnp.float32
    comps, layers, rows, cols = fine_field.shape
    crows, ccols = coarse_field.shape[2:]
    fine = pltpu.VMEM(fine_field.shape, f32)
    coarse = pltpu.VMEM(coarse_field.shape, f32)
    plane_f = pltpu.VMEM((comps, rows, cols), f32)
    plane_c = pltpu.VMEM((comps, crows, ccols), f32)
    line = pltpu.VMEM((1, 4), f32)
    corrections = pltpu.VMEM((2, rows + crows, LANES), f32)
    edge_outs = [
        pltpu.VMEM((comps * layers // 4, 8, cols + ccols), f32),
        pltpu.VMEM((comps * layers // 4, 8, cols + ccols), f32),
        pltpu.VMEM((rows + crows, LANES), f32),
        pltpu.VMEM((rows + crows, LANES), f32),
    ]
    tall = pltpu.VMEM((cols // LANES, 2 * comps * rows, LANES), f32)
    one_c = pltpu.VMEM((crows, ccols), f32)
    fixed_outs = [pltpu.VMEM((rows, cols), f32)] * 3 + [one_c, one_c]
    prep_outs = [plane_f, plane_f, pltpu.VMEM((2 * comps * crows, ccols), f32), plane_c]
    picks = np.zeros((cols, ccols), np.float32)
    picks[np.arange(cols), np.arange(cols) // 2] = 1.0
    narrow = jnp.asarray(np.tile(picks, (3, 1)), jnp.bfloat16)
    widen = jnp.asarray(np.tile(picks.T, (3, 1)), jnp.bfloat16)
    tables = (*lateral_tables(rows, cols), *lateral_tables(crows, ccols), widen, narrow)
    pack, unpack = column_tables(comps * layers)
    lat = pltpu.VMEM((2, comps, 256, cols), f32)
    tr, sh = fine_traction, coarse_shear

    uf, uc, *mine = call(
        load_kernel, (fine_field, coarse_field, pack), [fine, coarse] + edge_outs,
        scratch=[pltpu.VMEM(pack.shape, pack.dtype), pltpu.SemaphoreType.DMA((3, layers // 4))], hbm=(0, 1, 2),
    )
    theirs = exchange(mine)
    sp, me, cs = fine_speed, fine_metric, coarse_speed
    vf, vc, *prep = call(
        functools.partial(main_kernel, True), (uf, sp, me, uc, cs, tr, *tables), [fine, coarse, *fixed_outs, *prep_outs],
        scratch=[lat, tall], flops=40_000_000,
    )
    vf, vc, change0, *mine = call(
        fix_kernel,
        (vf, vc, pack, unpack, uf, fine_previous, sp, me, uc, coarse_previous, cs, tr, sh, widen, narrow, *prep[:-1], *theirs),
        [fine, coarse, line] + edge_outs, scratch=[tall, corrections], alias={0: 0, 1: 1}, flops=20_000_000,
    )
    pf, pc, uf, uc, fixed = uf, uc, vf, vc, prep[: len(fixed_outs)]
    theirs = exchange(mine)
    vf, vc, *prep = call(
        functools.partial(main_kernel, False), (uf, sp, me, uc, cs, tr, *tables, *fixed, pf, pc),
        [fine, coarse, *prep_outs],
        scratch=[lat, tall], flops=40_000_000,
    )
    ghost_f, ghost_c, change1, slots = call(
        interface_kernel, (unpack, uf, uc, cs, tr, sh, widen, narrow, *fixed, *prep[:-1], *theirs),
        [plane_f, plane_c, line, corrections], scratch=[tall], flops=10_000_000,
    )
    n = lax.axis_size(ALL)
    out_f, out_c, spread = call(
        last_kernel,
        (change0, change1, sp, me, cs, uf, uc, vf, vc, ghost_f, ghost_c, slots, *theirs),
        [pltpu.HBM(fine_field.shape, f32), pltpu.HBM(coarse_field.shape, f32), pltpu.VMEM((n, STEPS, 4), f32)],
        scratch=[fine, coarse, pltpu.SemaphoreType.DMA((layers + 1,))], flops=40_000_000,
    )
    return out_f, out_c, jnp.max(lax.all_to_all(spread, ALL, 0, 0, tiled=True), axis=0)


def solution(mesh):
    field = P(None, None, "gx", Y)
    layered = P(None, "gx", Y)
    plane = P("gx", Y)
    return jax.shard_map(
        on_device,
        mesh=mesh,
        in_specs=(field, field, layered, layered, field, field, layered, plane, plane),
        out_specs=(field, field, P()),
        check_vma=False,
    )
```

```python
import functools

import jax
import jax.numpy as jnp
import numpy as np
from jax import lax
from jax.experimental import pallas as pl
from jax.experimental.pallas import tpu as pltpu
from jax.sharding import PartitionSpec as P

STEPS = 2
LANES = 128
TWELFTH = 1.0 / 12.0
Y = ("grid", "gy")
ALL = ("grid", "gx", "gy")
VMEM_LIMIT = 16 << 20


def turn(x, by, axis):
    return pltpu.roll(x, by % x.shape[axis], axis)


def bands(length, copies):
    one = sum(w * np.eye(length, k=o) for o, w in ((1, 16.0), (-1, 16.0), (2, -1.0), (-2, -1.0)))
    return np.kron(np.eye(copies), one)


def lateral_tables(rows, cols):
    stack = 256 // rows
    left, right = bands(rows, stack), bands(cols, 1)
    return (
        jnp.asarray(np.concatenate([left, left], axis=1), jnp.bfloat16),
        jnp.asarray(np.concatenate([right, right], axis=0), jnp.bfloat16),
    )


def lateral12(planes, left, right):
    a = planes.astype(jnp.bfloat16)
    b = (planes - a.astype(jnp.float32)).astype(jnp.bfloat16)
    y = jnp.dot(jnp.concatenate([a, b], axis=1), right[...], preferred_element_type=jnp.float32)
    x = jnp.dot(left[...], jnp.concatenate([a, b], axis=0), preferred_element_type=jnp.float32)
    return (x + y) - 60.0 * planes


def depth12(ref, c, k):
    last = ref.shape[1] - 1

    def pair(offset):
        taps = [ref[c, k + o] for o in (-offset, offset) if not isinstance(k, int) or 0 <= k + o <= last]
        return taps[0] + taps[1] if len(taps) == 2 else taps[0]

    return 16.0 * pair(1) - pair(2) - 30.0 * ref[c, k]


def slot(p):
    return (p // 32) * LANES + (p % 32) * 4


def column_tables(planes):
    pack, unpack = np.zeros((2 * LANES, 2 * LANES)), np.zeros((2 * LANES, 2 * LANES))
    for p in range(planes):
        v0, v1, u0, u1 = (slot(p) + i for i in range(4))
        down, up = 2 * p, LANES + 2 * p
        pack[u0, down] = -1.0
        pack[u0, down + 1], pack[u1, down + 1] = 16.0, -1.0
        pack[v0, up], pack[v1, up] = -1.0, 16.0
        pack[v1, up + 1] = -1.0
        unpack[2 * p, slot(p) + 2] = unpack[2 * p + 1, slot(p) + 3] = 1.0
        unpack[LANES + 2 * p, slot(p)] = unpack[LANES + 2 * p + 1, slot(p) + 1] = 1.0
    return tuple(jnp.asarray(np.tile(t, (3, 1)), jnp.bfloat16) for t in (pack, unpack))


def pieces(x):
    a = x.astype(jnp.bfloat16)
    rest = x - a.astype(jnp.float32)
    b = rest.astype(jnp.bfloat16)
    c = (rest - b.astype(jnp.float32)).astype(jnp.bfloat16)
    return jnp.concatenate([a, b, c], axis=-1)


def times(x, table):
    return jnp.dot(pieces(x), table[...], preferred_element_type=jnp.float32)


def pack_rows(tops, bottoms, x_down, x_up):
    lanes = 0
    for top, bottom in zip(tops, bottoms):
        comps, layers, _, width = top.shape
        at = slice(lanes, lanes + width)
        lanes += width
        sub = lax.broadcasted_iota(jnp.int32, (8, width), 0)
        for c in range(comps):
            for g in range(0, layers, 4):
                first = last = jnp.zeros((8, width), jnp.float32)
                for i in range(4):
                    first = jnp.where(sub // 2 == i, turn(top[c, g + i], 2 * i, 0), first)
                    last = jnp.where(sub // 2 == i, turn(bottom[c, g + i], 2 * i + 2, 0), last)
                tile = (c * layers + g) // 4
                x_down[tile, :, at] = jnp.where(lax.rem(sub, 2) == 1, 16.0 * turn(first, 1, 0), 0.0) - first
                x_up[tile, :, at] = jnp.where(lax.rem(sub, 2) == 0, 16.0 * turn(last, -1, 0), 0.0) - last


def pack_columns(uf, uc, pack, y_down, y_up):
    raw = []
    for ref in (uf, uc):
        comps, layers, n, width = ref.shape
        lane = lax.broadcasted_iota(jnp.int32, (n, LANES), 1)
        columns = [jnp.zeros((n, LANES), jnp.float32) for _ in range(2)]
        for c in range(comps):
            for k in range(layers):
                p = c * layers + k
                u = ref[c, k, :, 0:LANES]
                if width > LANES:
                    u = jnp.where(lane < 2, u, ref[c, k, :, width - LANES : width])
                u = turn(u, slot(p) % LANES + 2, 1)
                half = slot(p) // LANES
                columns[half] = jnp.where(lane // 4 == slot(p) % LANES // 4, u, columns[half])
        raw.append(jnp.concatenate(columns, axis=1))
    packed = times(jnp.concatenate(raw, axis=0), pack)
    y_down[...] = packed[:, 0:LANES]
    y_up[...] = packed[:, LANES : 2 * LANES]


def rows_kernel(uf_hbm, uc_hbm, pack_hbm, x_down, x_up, pack, top_f, bottom_f, top_c, bottom_c, sem):
    table = pltpu.make_async_copy(pack_hbm, pack, sem.at[4])
    copies = []
    for ref, top, bottom in ((uf_hbm, top_f, bottom_f), (uc_hbm, top_c, bottom_c)):
        rows = ref.shape[2]
        for at, into in ((pl.ds(0, 8), top), (pl.ds(rows - 8, 8), bottom)):
            copies.append(pltpu.make_async_copy(ref.at[:, :, at], into, sem.at[len(copies)]))
            copies[-1].start()
    table.start()
    for copy in copies:
        copy.wait()
    pack_rows((top_f, top_c), (bottom_f, bottom_c), x_down, x_up)
    table.wait()


def columns_kernel(uf, uc, pack, y_down, y_up):
    pack_columns(uf, uc, pack, y_down, y_up)


def main_kernel(first_step, uf, sp, me, uc, cs, tr, left_f, right_f, left_c, right_c, widen, narrow, *refs):
    comps, layers, rows, cols = uf.shape
    crows, ccols = uc.shape[2:]
    size_f, size_c = 256 // rows, 256 // crows
    if first_step:
        vf, vc, *fixed, beta, first, sums, lat_c0, lat, tall = refs
    else:
        *fixed, pf, pc, vf, vc, beta, first, sums, lat_c0, lat, tall = refs

    def coarse(start):
        for c in range(comps):
            planes = uc[c, start : start + size_c].reshape(256, ccols)
            part = lateral12(planes, left_c, right_c)
            if start == 0:
                lat_c0[c] = part[0:crows, :]
            for i in range(size_c):
                k = start + i
                old = 2.0 * uc[c, k] if first_step else 2.0 * uc[c, k] - pc[c, k]
                vc[c, k] = old + cs[k] * TWELFTH * (part[i * crows : (i + 1) * crows, :] + depth12(uc, c, k))

    def fine_lateral(start):
        for c in range(comps):
            planes = uf[c, start : start + size_f].reshape(256, cols)
            lat[start // size_f % 2, c] = lateral12(planes, left_f, right_f)

    def fine(start):
        for i in range(size_f):
            k = start + i
            s12, m2 = sp[k] * TWELFTH, me[k] * me[k]
            for c in range(comps):
                old = 2.0 * uf[c, k] if first_step else 2.0 * uf[c, k] - pf[c, k]
                side = lat[start // size_f % 2, c, i * rows : (i + 1) * rows, :]
                vf[c, k] = old + s12 * (side + m2 * depth12(uf, c, k))

    fine_lateral(0)
    for start in range(0, layers, size_f):
        if start + size_f < layers:
            fine_lateral(start + size_f)
        fine(start)
    if first_step:
        prepare_fixed(sp, me, cs, tr, widen, narrow, tall, *fixed)
    lat_b = lat.at[(layers - 1) // size_f % 2, :, 256 - rows : 256]
    for start in range(0, layers, size_c):
        coarse(start)
    prepare(uf, uc, cs, tr, widen, narrow, lat_b, tall, *fixed, beta, first, sums, lat_c0)


class Edges:
    def __init__(self, got, slots, shapes, unpack=None):
        self.got_xd, self.got_xu, got_yd, got_yu = got
        self.slots = slots
        (self.layers, rows, cols), (crows, ccols) = shapes
        self.fine = (slice(0, rows), slice(0, cols), rows, cols)
        self.coarse = (slice(rows, rows + crows), slice(cols, cols + ccols), crows, ccols)
        x_at, x_n = lax.axis_index("gx"), lax.axis_size("gx")
        y_at, y_n = lax.axis_index(Y), lax.axis_size(Y)
        self.x_low, self.x_high = x_at > 0, x_at < x_n - 1
        if unpack is None:
            return
        up = jnp.where(y_at > 0, got_yu[...], 0.0)
        down = jnp.where(y_at < y_n - 1, got_yd[...], 0.0)
        both = times(jnp.concatenate([up, down], axis=1), unpack)
        slots[0] = both[:, 0:LANES]
        slots[1] = both[:, LANES : 2 * LANES]

    def plane(self, grid, c, g, i):
        ys, xs, n, width = grid
        p = c * self.layers + g + i
        lane = lax.broadcasted_iota(jnp.int32, (n, LANES), 1)
        sub = lax.broadcasted_iota(jnp.int32, (8, width), 0)
        half, quad = (p // 32, p % 32) if isinstance(p, int) else (lax.div(p, 32), lax.rem(p, 32))
        u = pltpu.roll(self.slots[half, ys, :], LANES - 2 - 4 * quad, 1)
        low, high = jnp.where(lane < 2, u, 0.0), jnp.where(lane >= LANES - 2, u, 0.0)
        if width == LANES:
            columns = low + high
        else:
            columns = jnp.concatenate([low, high], axis=1)
        tile = p // 4 if isinstance(p, int) else lax.div(c * self.layers + g, 4)
        first = jnp.where(jnp.logical_and(sub < 2, self.x_low), turn(self.got_xu[tile, :, xs], -2 * i, 0), 0.0)
        last = jnp.where(jnp.logical_and(sub >= 6, self.x_high), turn(self.got_xd[tile, :, xs], 6 - 2 * i, 0), 0.0)
        return jnp.concatenate([columns[0:8] + first, columns[8 : n - 8], columns[n - 8 : n] + last], axis=0)


def stretch(planes, widen, tall, rows, cols):
    wide = times(jnp.concatenate(planes, axis=0), widen)
    n = len(planes) * rows // 2
    halves = range(cols // LANES)
    for half in halves:
        part = wide[:, half * LANES : (half + 1) * LANES]
        tall[half, pl.ds(0, n, 2), :] = part
        tall[half, pl.ds(1, n, 2), :] = part
    return [
        jnp.concatenate([tall[half, i * rows : (i + 1) * rows, :] for half in halves], axis=1)
        for i in range(len(planes))
    ]


def row_pairs(planes, tall):
    rows, cols = planes[0].shape
    n = len(planes) * rows // 2
    halves = range(cols // LANES)
    for i, plane in enumerate(planes):
        for half in halves:
            tall[half, i * rows : (i + 1) * rows, :] = plane[:, half * LANES : (half + 1) * LANES]
    return tuple(
        jnp.concatenate([tall[half, pl.ds(start, n, 2), :] for half in halves], axis=1) for start in range(2)
    )


def prepare_fixed(sp, me, cs, tr, widen, narrow, tall, alpha_o, gain_o, metric_o, rate_o, top_o):
    rows, cols = tr.shape
    b = sp.shape[0] - 1
    s, m = sp[b], me[b]
    m2 = m * m
    gain = 1.0 / (s * m2)
    alpha = gain * stretch([cs[0]], widen, tall, rows, cols)[0]
    alpha_o[...] = alpha
    gain_o[...] = gain * (12.0 / 14.0)
    metric_o[...] = (1.0 / 14.0) / m2
    even_rows, odd_rows = row_pairs([tr[...] * alpha, alpha], tall)
    crows = rows // 2
    top = jnp.maximum(even_rows[crows:], odd_rows[crows:])
    top = jnp.maximum(top, turn(top, -1, 1))
    lane = lax.broadcasted_iota(jnp.int32, top.shape, 1)
    top = jnp.where(lax.rem(lane, 2) == 0, top, 0.0)
    both = times(jnp.concatenate([even_rows[:crows] + odd_rows[:crows], top], axis=0), narrow)
    rate_o[...] = both[:crows]
    top_o[...] = both[crows:]


def prepare(uf, uc, cs, tr, widen, narrow, lat_b, tall, alpha, gain14, metric14, rate, top, beta_o, first_o, sums_o, lat_c0):
    comps, layers, rows, cols = uf.shape
    b = layers - 1
    t = tr[...]
    c0 = [uc[c, 0] for c in range(comps)]
    pull = [
        cs[0] * (lat_c0[c] - 29.0 * uc[c, 0] + 16.0 * uc[c, 1] - uc[c, 2]) * TWELFTH for c in range(comps)
    ]
    wide = stretch(pull + c0, widen, tall, rows, cols)
    weighted = []
    for c in range(comps):
        ub, u1, u2 = uf[c, b], uf[c, b - 1], uf[c, b - 2]
        bc = gain14[...] * wide[c] - metric14[...] * lat_b[c] + (u2 - 16.0 * u1 + 29.0 * ub) * (1.0 / 14.0)
        beta_o[c] = bc
        first_o[c] = alpha[...] * wide[comps + c] - ub
        still = (u2 - 8.0 * u1 + ub) * TWELFTH
        weighted.append(t * (still + 0.5 * bc))
        weighted.append(t * (still + 0.5 * ub))
    even_rows, odd_rows = row_pairs(weighted, tall)
    sums_o[...] = times(even_rows + odd_rows, narrow)


def interface(edges, uc, cs, tr, sh, widen, narrow, tall, alpha, gain14, metric14, rate_in, top, beta_in, first_in, sums):
    comps, rows, cols = beta_in.shape
    crows, ccols = sh.shape
    layers = edges.layers
    inv_sh = 1.0 / sh[...]
    t = tr[...]
    pull = [cs[0] * TWELFTH * edges.plane(edges.coarse, c, 0, 0) for c in range(comps)]
    wide = stretch(pull, widen, tall, rows, cols)
    beta, weighted, first = [], [], None
    for c in range(comps):
        more = gain14[...] * wide[c] - metric14[...] * edges.plane(edges.fine, c, layers - 4, 3)
        bc = beta_in[c] + more
        beta.append(bc)
        weighted.append(0.5 * t * more)
        change = jnp.max(jnp.abs(first_in[c] + bc), axis=0, keepdims=True)
        first = change if first is None else jnp.maximum(first, change)
    even_rows, odd_rows = row_pairs(weighted, tall)
    more = times(even_rows + odd_rows, narrow)

    def part(i):
        return sums[i * crows : (i + 1) * crows, :]

    rate = rate_in[...] * (0.5 * inv_sh)
    history = [[], [], [], []]
    c3s, c4s = [], []
    for c in range(comps):
        c0 = uc[c, 0]
        q6 = (8.0 * uc[c, 1] - c0 - uc[c, 2]) * (1.0 / 6.0)
        base = q6 - (part(2 * c) + more[c * crows : (c + 1) * crows, :]) * inv_sh
        c1 = q6 - part(2 * c + 1) * inv_sh
        c2 = base - rate * c0
        c3 = base - rate * c1
        c4 = base - rate * c2
        d1, d2, d3, d4 = (jnp.abs(x) for x in (c1 - c0, c2 - c1, c3 - c2, c4 - c3))
        history[0].append(d1)
        history[1].append(jnp.maximum(d2, top[...] * d1))
        history[2].append(jnp.maximum(d3, top[...] * d2))
        history[3].append(jnp.maximum(d4, top[...] * d3))
        c3s.append(c3)
        c4s.append(c4)
    lane = lax.broadcasted_iota(jnp.int32, (1, LANES), 1)
    line = jnp.zeros((1, LANES), jnp.float32)
    for n in range(4):
        d = jnp.maximum(jnp.maximum(history[n][0], history[n][1]), history[n][2])
        d = jnp.max(d, axis=0, keepdims=True)
        if n == 0:
            for half in range(cols // LANES):
                d = jnp.maximum(d, first[:, half * LANES : (half + 1) * LANES])
        line = jnp.where(lane == n, jnp.max(d, axis=1, keepdims=True), line)
    wide = stretch(c3s, widen, tall, rows, cols)
    return [alpha[...] * wide[c] + beta[c] for c in range(comps)], c4s, line[:, 0:4]


PREP = 8


def fix_kernel(vf_in, vc_in, pack, unpack, uf, pf, sp, me, uc, pc, cs, tr, sh, widen, narrow, *refs):
    prep, got = refs[:PREP], refs[PREP : PREP + 4]
    vf, vc, change, *packed = refs[PREP + 4 : -2]
    tall, slots = refs[-2:]
    comps, layers, rows, cols = uf.shape
    edges = Edges(got, slots, (uf.shape[1:], uc.shape[2:]), unpack)
    ghost_f, ghost_c, line = interface(edges, uc, cs, tr, sh, widen, narrow, tall, *prep)
    change[...] = line
    b = layers - 1
    s_last = sp[b] * me[b] * me[b] * TWELFTH
    s_next = sp[b - 1] * me[b - 1] * me[b - 1] * TWELFTH
    for c in range(comps):
        vf[c, b] = vf_in[c, b] + s_last * (14.0 * ghost_f[c] + uf[c, b])
        vf[c, b - 1] = vf_in[c, b - 1] - s_next * ghost_f[c]
        vc[c, 0] = vc_in[c, 0] + cs[0] * TWELFTH * (14.0 * ghost_c[c] + uc[c, 0])
        vc[c, 1] = vc_in[c, 1] - cs[1] * TWELFTH * ghost_c[c]

    for g in range(0, layers, 4):
        for i in range(4):
            s12, cs12 = sp[g + i] * TWELFTH, cs[g + i] * TWELFTH
            for c in range(comps):
                vf[c, g + i] = vf_in[c, g + i] - pf[c, g + i] + s12 * edges.plane(edges.fine, c, g, i)
                vc[c, g + i] = vc_in[c, g + i] - pc[c, g + i] + cs12 * edges.plane(edges.coarse, c, g, i)

    pack_columns(vf, vc, pack, *packed[2:])
    tops = [v.at[:, :, 0:8] for v in (vf, vc)]
    bottoms = [v.at[:, :, v.shape[2] - 8 : v.shape[2]] for v in (vf, vc)]
    pack_rows(tops, bottoms, *packed[:2])


def interface_kernel(unpack, uf, uc, cs, tr, sh, widen, narrow, *refs):
    prep, got = refs[:PREP], refs[PREP : PREP + 4]
    ghost_f, ghost_c, change, slots, tall = refs[PREP + 4 :]
    edges = Edges(got, slots, (uf.shape[1:], uc.shape[2:]), unpack)
    g, c4, line = interface(edges, uc, cs, tr, sh, widen, narrow, tall, *prep)
    for c in range(uf.shape[0]):
        ghost_f[c] = g[c]
        ghost_c[c] = c4[c]
    change[...] = line


def last_kernel(change0, change1, sp, me, cs, uf, uc, vf, vc, ghost_f, ghost_c, slots, *refs):
    got = refs[0:4]
    out_f, out_c, spread, done_f, done_c, sem = refs[4:]
    comps, layers, rows, cols = uf.shape
    b = layers - 1
    edges = Edges(got, slots, (uf.shape[1:], uc.shape[2:]))
    for step, line in enumerate((change0, change1)):
        spread[:, step : step + 1, :] = jnp.broadcast_to(line[...][None], (spread.shape[0], 1, spread.shape[2]))

    def copy(k):
        return pltpu.make_async_copy(done_f.at[:, k], out_f.at[:, k], sem.at[k])

    copy_coarse = pltpu.make_async_copy(done_c, out_c, sem.at[layers])

    def fine(k, g, i):
        s12 = sp[k] * TWELFTH
        for c in range(comps):
            total = edges.plane(edges.fine, c, g, i)
            if isinstance(k, int) and k == b:
                total = total + me[k] * me[k] * (14.0 * ghost_f[c] + uf[c, b])
            if isinstance(k, int) and k == b - 1:
                total = total - me[k] * me[k] * ghost_f[c]
            done_f[c, k] = vf[c, k] + s12 * total
        copy(k).start()

    for k in range(layers):
        fine(k, k // 4 * 4, k % 4)

    for g in range(0, layers, 4):
        for i in range(4):
            cs12 = cs[g + i] * TWELFTH
            for c in range(comps):
                done_c[c, g + i] = vc[c, g + i] + cs12 * edges.plane(edges.coarse, c, g, i)

    for c in range(comps):
        done_c[c, 0] = done_c[c, 0] + cs[0] * TWELFTH * (14.0 * ghost_c[c] + uc[c, 0])
        done_c[c, 1] = done_c[c, 1] - cs[1] * TWELFTH * ghost_c[c]
    copy_coarse.start()
    for k in range(layers):
        copy(k).wait()
    copy_coarse.wait()


def call(kernel, args, outs, scratch=(), alias={}, flops=0, hbm=()):
    spaces = [pltpu.HBM if i in hbm else pltpu.VMEM for i in range(len(args))]
    return pl.pallas_call(
        kernel,
        out_shape=tuple(outs),
        in_specs=[pl.BlockSpec(memory_space=s) for s in spaces],
        out_specs=tuple(pl.BlockSpec(memory_space=o.memory_space) for o in outs),
        scratch_shapes=list(scratch),
        input_output_aliases=alias,
        cost_estimate=pl.CostEstimate(flops=flops, bytes_accessed=flops, transcendentals=0),
        compiler_params=pltpu.CompilerParams(vmem_limit_bytes=VMEM_LIMIT),
    )(*[pltpu.with_memory_space_constraint(x, s) for x, s in zip(args, spaces)])


def exchange(parts):
    x_down, x_up, y_down, y_up = parts

    def ring(value, axis, by):
        n = lax.axis_size(axis)
        return lax.ppermute(value, axis, [(i, (i + by) % n) for i in range(n)])

    return (ring(x_down, "gx", -1), ring(x_up, "gx", 1), ring(y_down, Y, -1), ring(y_up, Y, 1))


def on_device(
    fine_field, fine_previous, fine_speed, fine_metric, coarse_field, coarse_previous, coarse_speed,
    fine_traction, coarse_shear,
):
    f32 = jnp.float32
    comps, layers, rows, cols = fine_field.shape
    crows, ccols = coarse_field.shape[2:]
    fine = pltpu.VMEM(fine_field.shape, f32)
    coarse = pltpu.VMEM(coarse_field.shape, f32)
    plane_f = pltpu.VMEM((comps, rows, cols), f32)
    plane_c = pltpu.VMEM((comps, crows, ccols), f32)
    line = pltpu.VMEM((1, 4), f32)
    corrections = pltpu.VMEM((2, rows + crows, LANES), f32)
    edge_outs = [
        pltpu.VMEM((comps * layers // 4, 8, cols + ccols), f32),
        pltpu.VMEM((comps * layers // 4, 8, cols + ccols), f32),
        pltpu.VMEM((rows + crows, LANES), f32),
        pltpu.VMEM((rows + crows, LANES), f32),
    ]
    tall = pltpu.VMEM((cols // LANES, 2 * comps * rows + 8, LANES), f32)
    one_c = pltpu.VMEM((crows, ccols), f32)
    fixed_outs = [pltpu.VMEM((rows, cols), f32)] * 3 + [one_c, one_c]
    prep_outs = [plane_f, plane_f, pltpu.VMEM((2 * comps * crows, ccols), f32), plane_c]
    picks = np.zeros((cols, ccols), np.float32)
    picks[np.arange(cols), np.arange(cols) // 2] = 1.0
    narrow = jnp.asarray(np.tile(picks, (3, 1)), jnp.bfloat16)
    widen = jnp.asarray(np.tile(picks.T, (3, 1)), jnp.bfloat16)
    tables = (*lateral_tables(rows, cols), *lateral_tables(crows, ccols), widen, narrow)
    pack, unpack = column_tables(comps * layers)
    lat = pltpu.VMEM((2, comps, 256, cols), f32)
    tr, sh = fine_traction, coarse_shear

    uf, uc = fine_field, coarse_field
    ends = [pltpu.VMEM((*x.shape[:2], 8, x.shape[3]), f32) for x in (uf, uf, uc, uc)]
    x_down, x_up, pack = call(
        rows_kernel, (uf, uc, pack), [*edge_outs[:2], pltpu.VMEM(pack.shape, pack.dtype)],
        scratch=[*ends, pltpu.SemaphoreType.DMA((5,))], hbm=(0, 1, 2),
    )
    mine = (x_down, x_up, *call(columns_kernel, (uf, uc, pack), edge_outs[2:]))
    theirs = exchange(mine)
    sp, me, cs = fine_speed, fine_metric, coarse_speed
    vf, vc, *prep = call(
        functools.partial(main_kernel, True), (uf, sp, me, uc, cs, tr, *tables), [fine, coarse, *fixed_outs, *prep_outs],
        scratch=[lat, tall], flops=40_000_000,
    )
    vf, vc, change0, *mine = call(
        fix_kernel,
        (vf, vc, pack, unpack, uf, fine_previous, sp, me, uc, coarse_previous, cs, tr, sh, widen, narrow, *prep[:-1], *theirs),
        [fine, coarse, line] + edge_outs, scratch=[tall, corrections], alias={0: 0, 1: 1}, flops=20_000_000,
    )
    pf, pc, uf, uc, fixed = uf, uc, vf, vc, prep[: len(fixed_outs)]
    theirs = exchange(mine)
    vf, vc, *prep = call(
        functools.partial(main_kernel, False), (uf, sp, me, uc, cs, tr, *tables, *fixed, pf, pc),
        [fine, coarse, *prep_outs],
        scratch=[lat, tall], flops=40_000_000,
    )
    ghost_f, ghost_c, change1, slots = call(
        interface_kernel, (unpack, uf, uc, cs, tr, sh, widen, narrow, *fixed, *prep[:-1], *theirs),
        [plane_f, plane_c, line, corrections], scratch=[tall], flops=10_000_000,
    )
    n = lax.axis_size(ALL)
    out_f, out_c, spread = call(
        last_kernel,
        (change0, change1, sp, me, cs, uf, uc, vf, vc, ghost_f, ghost_c, slots, *theirs),
        [pltpu.HBM(fine_field.shape, f32), pltpu.HBM(coarse_field.shape, f32), pltpu.VMEM((n, STEPS, 4), f32)],
        scratch=[fine, coarse, pltpu.SemaphoreType.DMA((layers + 1,))], flops=40_000_000,
    )
    return out_f, out_c, jnp.max(lax.all_to_all(spread, ALL, 0, 0, tiled=True), axis=0)


def solution(mesh):
    field = P(None, None, "gx", Y)
    layered = P(None, "gx", Y)
    plane = P("gx", Y)
    return jax.shard_map(
        on_device,
        mesh=mesh,
        in_specs=(field, field, layered, layered, field, field, layered, plane, plane),
        out_specs=(field, field, P()),
        check_vma=False,
    )
```

```python
import functools

import jax
import jax.numpy as jnp
import numpy as np
from jax import lax
from jax.experimental import pallas as pl
from jax.experimental.pallas import tpu as pltpu
from jax.sharding import PartitionSpec as P

STEPS = 2
LANES = 128
TWELFTH = 1.0 / 12.0
Y = ("grid", "gy")
ALL = ("grid", "gx", "gy")
VMEM_LIMIT = 16 << 20


def turn(x, by, axis):
    return pltpu.roll(x, by % x.shape[axis], axis)


def bands(length, copies):
    one = sum(w * np.eye(length, k=o) for o, w in ((1, 16.0), (-1, 16.0), (2, -1.0), (-2, -1.0)))
    return np.kron(np.eye(copies), one)


def lateral_tables(rows, cols):
    stack = 256 // rows
    left, right = bands(rows, stack), bands(cols, 1)
    return (
        jnp.asarray(np.concatenate([left, left], axis=1), jnp.bfloat16),
        jnp.asarray(np.concatenate([right, right], axis=0), jnp.bfloat16),
    )


def lateral12(planes, left, right):
    a = planes.astype(jnp.bfloat16)
    b = (planes - a.astype(jnp.float32)).astype(jnp.bfloat16)
    y = jnp.dot(jnp.concatenate([a, b], axis=1), right[...], preferred_element_type=jnp.float32)
    x = jnp.dot(left[...], jnp.concatenate([a, b], axis=0), preferred_element_type=jnp.float32)
    return (x + y) - 60.0 * planes


def depth12(ref, c, k):
    last = ref.shape[1] - 1

    def pair(offset):
        taps = [ref[c, k + o] for o in (-offset, offset) if not isinstance(k, int) or 0 <= k + o <= last]
        return taps[0] + taps[1] if len(taps) == 2 else taps[0]

    return 16.0 * pair(1) - pair(2) - 30.0 * ref[c, k]


def slot(p):
    return (p // 32) * LANES + (p % 32) * 4


def column_tables(planes):
    pack, unpack = np.zeros((2 * LANES, 2 * LANES)), np.zeros((2 * LANES, 2 * LANES))
    for p in range(planes):
        v0, v1, u0, u1 = (slot(p) + i for i in range(4))
        down, up = 2 * p, LANES + 2 * p
        pack[u0, down] = -1.0
        pack[u0, down + 1], pack[u1, down + 1] = 16.0, -1.0
        pack[v0, up], pack[v1, up] = -1.0, 16.0
        pack[v1, up + 1] = -1.0
        unpack[2 * p, slot(p) + 2] = unpack[2 * p + 1, slot(p) + 3] = 1.0
        unpack[LANES + 2 * p, slot(p)] = unpack[LANES + 2 * p + 1, slot(p) + 1] = 1.0
    return tuple(jnp.asarray(np.tile(t, (3, 1)), jnp.bfloat16) for t in (pack, unpack))


def pieces(x):
    a = x.astype(jnp.bfloat16)
    rest = x - a.astype(jnp.float32)
    b = rest.astype(jnp.bfloat16)
    c = (rest - b.astype(jnp.float32)).astype(jnp.bfloat16)
    return jnp.concatenate([a, b, c], axis=-1)


def times(x, table):
    return jnp.dot(pieces(x), table[...], preferred_element_type=jnp.float32)


def pack_rows(tops, bottoms, x_down, x_up):
    lanes = 0
    for top, bottom in zip(tops, bottoms):
        comps, layers, _, width = top.shape
        at = slice(lanes, lanes + width)
        lanes += width
        sub = lax.broadcasted_iota(jnp.int32, (8, width), 0)
        for c in range(comps):
            for g in range(0, layers, 4):
                first = last = jnp.zeros((8, width), jnp.float32)
                for i in range(4):
                    first = jnp.where(sub // 2 == i, turn(top[c, g + i], 2 * i, 0), first)
                    last = jnp.where(sub // 2 == i, turn(bottom[c, g + i], 2 * i + 2, 0), last)
                tile = (c * layers + g) // 4
                x_down[tile, :, at] = jnp.where(lax.rem(sub, 2) == 1, 16.0 * turn(first, 1, 0), 0.0) - first
                x_up[tile, :, at] = jnp.where(lax.rem(sub, 2) == 0, 16.0 * turn(last, -1, 0), 0.0) - last


def pack_columns(uf, uc, pack, y_down, y_up):
    raw = []
    for ref in (uf, uc):
        comps, layers, n, width = ref.shape
        lane = lax.broadcasted_iota(jnp.int32, (n, LANES), 1)
        columns = [jnp.zeros((n, LANES), jnp.float32) for _ in range(2)]
        for c in range(comps):
            for k in range(layers):
                p = c * layers + k
                u = ref[c, k, :, 0:LANES]
                if width > LANES:
                    u = jnp.where(lane < 2, u, ref[c, k, :, width - LANES : width])
                u = turn(u, slot(p) % LANES + 2, 1)
                half = slot(p) // LANES
                columns[half] = jnp.where(lane // 4 == slot(p) % LANES // 4, u, columns[half])
        raw.append(jnp.concatenate(columns, axis=1))
    packed = times(jnp.concatenate(raw, axis=0), pack)
    y_down[...] = packed[:, 0:LANES]
    y_up[...] = packed[:, LANES : 2 * LANES]


def rows_kernel(uf_hbm, uc_hbm, pack_hbm, x_down, x_up, pack, top_f, bottom_f, top_c, bottom_c, sem):
    table = pltpu.make_async_copy(pack_hbm, pack, sem.at[4])
    copies = []
    for ref, top, bottom in ((uf_hbm, top_f, bottom_f), (uc_hbm, top_c, bottom_c)):
        rows = ref.shape[2]
        for at, into in ((pl.ds(0, 8), top), (pl.ds(rows - 8, 8), bottom)):
            copies.append(pltpu.make_async_copy(ref.at[:, :, at], into, sem.at[len(copies)]))
            copies[-1].start()
    table.start()
    for copy in copies:
        copy.wait()
    pack_rows((top_f, top_c), (bottom_f, bottom_c), x_down, x_up)
    table.wait()


def columns_kernel(uf, uc, pack, y_down, y_up):
    pack_columns(uf, uc, pack, y_down, y_up)


def main_kernel(first_step, uf, sp, me, uc, cs, tr, left_f, right_f, left_c, right_c, widen, narrow, *refs):
    comps, layers, rows, cols = uf.shape
    crows, ccols = uc.shape[2:]
    size_f, size_c = 256 // rows, 256 // crows
    if first_step:
        vf, vc, *fixed, beta, first, sums, lat_c0, lat, tall = refs
    else:
        *fixed, pf, pc, vf, vc, beta, first, sums, lat_c0, lat, tall = refs

    def coarse(start):
        for c in range(comps):
            planes = uc[c, start : start + size_c].reshape(256, ccols)
            part = lateral12(planes, left_c, right_c)
            if start == 0:
                lat_c0[c] = part[0:crows, :]
            for i in range(size_c):
                k = start + i
                old = 2.0 * uc[c, k] if first_step else 2.0 * uc[c, k] - pc[c, k]
                vc[c, k] = old + cs[k] * TWELFTH * (part[i * crows : (i + 1) * crows, :] + depth12(uc, c, k))

    def fine_lateral(start):
        for c in range(comps):
            planes = uf[c, start : start + size_f].reshape(256, cols)
            lat[start // size_f % 2, c] = lateral12(planes, left_f, right_f)

    def fine(start):
        for i in range(size_f):
            k = start + i
            s12, m2 = sp[k] * TWELFTH, me[k] * me[k]
            for c in range(comps):
                old = 2.0 * uf[c, k] if first_step else 2.0 * uf[c, k] - pf[c, k]
                side = lat[start // size_f % 2, c, i * rows : (i + 1) * rows, :]
                vf[c, k] = old + s12 * (side + m2 * depth12(uf, c, k))

    fine_lateral(0)
    for start in range(0, layers, size_f):
        if start + size_f < layers:
            fine_lateral(start + size_f)
        fine(start)
    if first_step:
        prepare_fixed(sp, me, cs, tr, widen, narrow, tall, *fixed)
    lat_b = lat.at[(layers - 1) // size_f % 2, :, 256 - rows : 256]
    for start in range(0, layers, size_c):
        coarse(start)
    prepare(uf, uc, cs, tr, widen, narrow, lat_b, tall, *fixed, beta, first, sums, lat_c0)


class Edges:
    def __init__(self, got, slots, shapes, unpack=None):
        self.got_xd, self.got_xu, got_yd, got_yu = got
        self.slots = slots
        (self.layers, rows, cols), (crows, ccols) = shapes
        self.fine = (slice(0, rows), slice(0, cols), rows, cols)
        self.coarse = (slice(rows, rows + crows), slice(cols, cols + ccols), crows, ccols)
        x_at, x_n = lax.axis_index("gx"), lax.axis_size("gx")
        y_at, y_n = lax.axis_index(Y), lax.axis_size(Y)
        self.x_low, self.x_high = x_at > 0, x_at < x_n - 1
        if unpack is None:
            return
        up = jnp.where(y_at > 0, got_yu[...], 0.0)
        down = jnp.where(y_at < y_n - 1, got_yd[...], 0.0)
        both = times(jnp.concatenate([up, down], axis=1), unpack)
        slots[0] = both[:, 0:LANES]
        slots[1] = both[:, LANES : 2 * LANES]

    def plane(self, grid, c, g, i):
        ys, xs, n, width = grid
        p = c * self.layers + g + i
        lane = lax.broadcasted_iota(jnp.int32, (n, LANES), 1)
        sub = lax.broadcasted_iota(jnp.int32, (8, width), 0)
        half, quad = (p // 32, p % 32) if isinstance(p, int) else (lax.div(p, 32), lax.rem(p, 32))
        u = pltpu.roll(self.slots[half, ys, :], LANES - 2 - 4 * quad, 1)
        low, high = jnp.where(lane < 2, u, 0.0), jnp.where(lane >= LANES - 2, u, 0.0)
        if width == LANES:
            columns = low + high
        else:
            columns = jnp.concatenate([low, high], axis=1)
        tile = p // 4 if isinstance(p, int) else lax.div(c * self.layers + g, 4)
        first = jnp.where(jnp.logical_and(sub < 2, self.x_low), turn(self.got_xu[tile, :, xs], -2 * i, 0), 0.0)
        last = jnp.where(jnp.logical_and(sub >= 6, self.x_high), turn(self.got_xd[tile, :, xs], 6 - 2 * i, 0), 0.0)
        return jnp.concatenate([columns[0:8] + first, columns[8 : n - 8], columns[n - 8 : n] + last], axis=0)


def stretch(planes, widen, tall, rows, cols):
    wide = times(jnp.concatenate(planes, axis=0), widen)
    n = len(planes) * rows // 2
    halves = range(cols // LANES)
    for half in halves:
        part = wide[:, half * LANES : (half + 1) * LANES]
        tall[half, pl.ds(0, n, 2), :] = part
        tall[half, pl.ds(1, n, 2), :] = part
    return [
        jnp.concatenate([tall[half, i * rows : (i + 1) * rows, :] for half in halves], axis=1)
        for i in range(len(planes))
    ]


def row_pairs(planes, tall):
    rows, cols = planes[0].shape
    n = len(planes) * rows // 2
    halves = range(cols // LANES)
    for i, plane in enumerate(planes):
        for half in halves:
            tall[half, i * rows : (i + 1) * rows, :] = plane[:, half * LANES : (half + 1) * LANES]
    return tuple(
        jnp.concatenate([tall[half, pl.ds(start, n, 2), :] for half in halves], axis=1) for start in range(2)
    )


def prepare_fixed(sp, me, cs, tr, widen, narrow, tall, alpha_o, gain_o, metric_o, rate_o, top_o):
    rows, cols = tr.shape
    b = sp.shape[0] - 1
    s, m = sp[b], me[b]
    m2 = m * m
    gain = 1.0 / (s * m2)
    alpha = gain * stretch([cs[0]], widen, tall, rows, cols)[0]
    alpha_o[...] = alpha
    gain_o[...] = gain * (12.0 / 14.0)
    metric_o[...] = (1.0 / 14.0) / m2
    even_rows, odd_rows = row_pairs([tr[...] * alpha, alpha], tall)
    crows = rows // 2
    top = jnp.maximum(even_rows[crows:], odd_rows[crows:])
    top = jnp.maximum(top, turn(top, -1, 1))
    lane = lax.broadcasted_iota(jnp.int32, top.shape, 1)
    top = jnp.where(lax.rem(lane, 2) == 0, top, 0.0)
    both = times(jnp.concatenate([even_rows[:crows] + odd_rows[:crows], top], axis=0), narrow)
    rate_o[...] = both[:crows]
    top_o[...] = both[crows:]


def prepare(uf, uc, cs, tr, widen, narrow, lat_b, tall, alpha, gain14, metric14, rate, top, beta_o, first_o, sums_o, lat_c0):
    comps, layers, rows, cols = uf.shape
    b = layers - 1
    t = tr[...]
    c0 = [uc[c, 0] for c in range(comps)]
    pull = [
        cs[0] * (lat_c0[c] - 29.0 * uc[c, 0] + 16.0 * uc[c, 1] - uc[c, 2]) * TWELFTH for c in range(comps)
    ]
    wide = stretch(pull + c0, widen, tall, rows, cols)
    weighted = []
    for c in range(comps):
        ub, u1, u2 = uf[c, b], uf[c, b - 1], uf[c, b - 2]
        bc = gain14[...] * wide[c] - metric14[...] * lat_b[c] + (u2 - 16.0 * u1 + 29.0 * ub) * (1.0 / 14.0)
        beta_o[c] = bc
        first_o[c] = alpha[...] * wide[comps + c] - ub
        still = (u2 - 8.0 * u1 + ub) * TWELFTH
        weighted.append(t * (still + 0.5 * bc))
        weighted.append(t * (still + 0.5 * ub))
    even_rows, odd_rows = row_pairs(weighted, tall)
    sums_o[...] = times(even_rows + odd_rows, narrow)


def interface(edges, uc, cs, tr, sh, widen, narrow, tall, alpha, gain14, metric14, rate_in, top, beta_in, first_in, sums):
    comps, rows, cols = beta_in.shape
    crows, ccols = sh.shape
    layers = edges.layers
    inv_sh = 1.0 / sh[...]
    t = tr[...]
    pull = [cs[0] * TWELFTH * edges.plane(edges.coarse, c, 0, 0) for c in range(comps)]
    wide = stretch(pull, widen, tall, rows, cols)
    beta, weighted, first = [], [], None
    for c in range(comps):
        more = gain14[...] * wide[c] - metric14[...] * edges.plane(edges.fine, c, layers - 4, 3)
        bc = beta_in[c] + more
        beta.append(bc)
        weighted.append(0.5 * t * more)
        change = jnp.max(jnp.abs(first_in[c] + bc), axis=0, keepdims=True)
        first = change if first is None else jnp.maximum(first, change)
    even_rows, odd_rows = row_pairs(weighted, tall)
    more = times(even_rows + odd_rows, narrow)

    def part(i):
        return sums[i * crows : (i + 1) * crows, :]

    rate = rate_in[...] * (0.5 * inv_sh)
    history = [[], [], [], []]
    c3s, c4s = [], []
    for c in range(comps):
        c0 = uc[c, 0]
        q6 = (8.0 * uc[c, 1] - c0 - uc[c, 2]) * (1.0 / 6.0)
        base = q6 - (part(2 * c) + more[c * crows : (c + 1) * crows, :]) * inv_sh
        c1 = q6 - part(2 * c + 1) * inv_sh
        c2 = base - rate * c0
        c3 = base - rate * c1
        c4 = base - rate * c2
        d1, d2, d3, d4 = (jnp.abs(x) for x in (c1 - c0, c2 - c1, c3 - c2, c4 - c3))
        history[0].append(d1)
        history[1].append(jnp.maximum(d2, top[...] * d1))
        history[2].append(jnp.maximum(d3, top[...] * d2))
        history[3].append(jnp.maximum(d4, top[...] * d3))
        c3s.append(c3)
        c4s.append(c4)
    lane = lax.broadcasted_iota(jnp.int32, (1, LANES), 1)
    line = jnp.zeros((1, LANES), jnp.float32)
    for n in range(4):
        d = jnp.maximum(jnp.maximum(history[n][0], history[n][1]), history[n][2])
        d = jnp.max(d, axis=0, keepdims=True)
        if n == 0:
            for half in range(cols // LANES):
                d = jnp.maximum(d, first[:, half * LANES : (half + 1) * LANES])
        line = jnp.where(lane == n, jnp.max(d, axis=1, keepdims=True), line)
    wide = stretch(c3s, widen, tall, rows, cols)
    return [alpha[...] * wide[c] + beta[c] for c in range(comps)], c4s, line[:, 0:4]


PREP = 8


def fix_kernel(vf_in, vc_in, pack, unpack, uf, pf, sp, me, uc, pc, cs, tr, sh, widen, narrow, *refs):
    prep, got = refs[:PREP], refs[PREP : PREP + 4]
    vf, vc, change, *packed = refs[PREP + 4 : -2]
    tall, slots = refs[-2:]
    comps, layers, rows, cols = uf.shape
    edges = Edges(got, slots, (uf.shape[1:], uc.shape[2:]), unpack)
    ghost_f, ghost_c, line = interface(edges, uc, cs, tr, sh, widen, narrow, tall, *prep)
    change[...] = line
    b = layers - 1
    s_last = sp[b] * me[b] * me[b] * TWELFTH
    s_next = sp[b - 1] * me[b - 1] * me[b - 1] * TWELFTH
    for c in range(comps):
        vf[c, b] = vf_in[c, b] + s_last * (14.0 * ghost_f[c] + uf[c, b])
        vf[c, b - 1] = vf_in[c, b - 1] - s_next * ghost_f[c]
        vc[c, 0] = vc_in[c, 0] + cs[0] * TWELFTH * (14.0 * ghost_c[c] + uc[c, 0])
        vc[c, 1] = vc_in[c, 1] - cs[1] * TWELFTH * ghost_c[c]

    for g in range(0, layers, 4):
        for i in range(4):
            s12, cs12 = sp[g + i] * TWELFTH, cs[g + i] * TWELFTH
            for c in range(comps):
                vf[c, g + i] = vf_in[c, g + i] - pf[c, g + i] + s12 * edges.plane(edges.fine, c, g, i)
                vc[c, g + i] = vc_in[c, g + i] - pc[c, g + i] + cs12 * edges.plane(edges.coarse, c, g, i)

    pack_columns(vf, vc, pack, *packed[2:])
    tops = [v.at[:, :, 0:8] for v in (vf, vc)]
    bottoms = [v.at[:, :, v.shape[2] - 8 : v.shape[2]] for v in (vf, vc)]
    pack_rows(tops, bottoms, *packed[:2])


def last_kernel(change0, unpack, sp, me, cs, uf, uc, vf, vc, tr, sh, widen, narrow, *refs):
    prep, got = refs[:PREP], refs[PREP : PREP + 4]
    out_f, out_c, spread, done_f, done_c, tall, slots, sem = refs[PREP + 4 :]
    comps, layers, rows, cols = uf.shape
    b = layers - 1
    edges = Edges(got, slots, (uf.shape[1:], uc.shape[2:]), unpack)

    def copy(k):
        return pltpu.make_async_copy(done_f.at[:, k], out_f.at[:, k], sem.at[k])

    copy_coarse = pltpu.make_async_copy(done_c, out_c, sem.at[layers])

    def fine(k):
        s12 = sp[k] * TWELFTH
        for c in range(comps):
            done_f[c, k] = vf[c, k] + s12 * edges.plane(edges.fine, c, k // 4 * 4, k % 4)

    for k in range(b - 1):
        fine(k)
        copy(k).start()
    ghost_f, ghost_c, line = interface(edges, uc, cs, tr, sh, widen, narrow, tall, *prep)
    for step, change in enumerate((change0[...], line)):
        spread[:, step : step + 1, :] = jnp.broadcast_to(change[None], (spread.shape[0], 1, spread.shape[2]))
    for k in (b - 1, b):
        fine(k)
        scale = sp[k] * me[k] * me[k] * TWELFTH
        for c in range(comps):
            more = 14.0 * ghost_f[c] + uf[c, b] if k == b else -ghost_f[c]
            done_f[c, k] = done_f[c, k] + scale * more
        copy(k).start()
    for k in range(layers):
        cs12 = cs[k] * TWELFTH
        for c in range(comps):
            total = edges.plane(edges.coarse, c, k // 4 * 4, k % 4)
            if k == 0:
                total = total + 14.0 * ghost_c[c] + uc[c, 0]
            if k == 1:
                total = total - ghost_c[c]
            done_c[c, k] = vc[c, k] + cs12 * total
    copy_coarse.start()
    for k in range(layers):
        copy(k).wait()
    copy_coarse.wait()


def call(kernel, args, outs, scratch=(), alias={}, flops=0, hbm=()):
    spaces = [pltpu.HBM if i in hbm else pltpu.VMEM for i in range(len(args))]
    return pl.pallas_call(
        kernel,
        out_shape=tuple(outs),
        in_specs=[pl.BlockSpec(memory_space=s) for s in spaces],
        out_specs=tuple(pl.BlockSpec(memory_space=o.memory_space) for o in outs),
        scratch_shapes=list(scratch),
        input_output_aliases=alias,
        cost_estimate=pl.CostEstimate(flops=flops, bytes_accessed=flops, transcendentals=0),
        compiler_params=pltpu.CompilerParams(vmem_limit_bytes=VMEM_LIMIT),
    )(*[pltpu.with_memory_space_constraint(x, s) for x, s in zip(args, spaces)])


def exchange(parts):
    x_down, x_up, y_down, y_up = parts

    def ring(value, axis, by):
        n = lax.axis_size(axis)
        return lax.ppermute(value, axis, [(i, (i + by) % n) for i in range(n)])

    return (ring(x_down, "gx", -1), ring(x_up, "gx", 1), ring(y_down, Y, -1), ring(y_up, Y, 1))


def on_device(
    fine_field, fine_previous, fine_speed, fine_metric, coarse_field, coarse_previous, coarse_speed,
    fine_traction, coarse_shear,
):
    f32 = jnp.float32
    comps, layers, rows, cols = fine_field.shape
    crows, ccols = coarse_field.shape[2:]
    fine = pltpu.VMEM(fine_field.shape, f32)
    coarse = pltpu.VMEM(coarse_field.shape, f32)
    plane_f = pltpu.VMEM((comps, rows, cols), f32)
    plane_c = pltpu.VMEM((comps, crows, ccols), f32)
    line = pltpu.VMEM((1, 4), f32)
    corrections = pltpu.VMEM((2, rows + crows, LANES), f32)
    edge_outs = [
        pltpu.VMEM((comps * layers // 4, 8, cols + ccols), f32),
        pltpu.VMEM((comps * layers // 4, 8, cols + ccols), f32),
        pltpu.VMEM((rows + crows, LANES), f32),
        pltpu.VMEM((rows + crows, LANES), f32),
    ]
    tall = pltpu.VMEM((cols // LANES, 2 * comps * rows + 8, LANES), f32)
    one_c = pltpu.VMEM((crows, ccols), f32)
    fixed_outs = [pltpu.VMEM((rows, cols), f32)] * 3 + [one_c, one_c]
    prep_outs = [plane_f, plane_f, pltpu.VMEM((2 * comps * crows, ccols), f32), plane_c]
    picks = np.zeros((cols, ccols), np.float32)
    picks[np.arange(cols), np.arange(cols) // 2] = 1.0
    narrow = jnp.asarray(np.tile(picks, (3, 1)), jnp.bfloat16)
    widen = jnp.asarray(np.tile(picks.T, (3, 1)), jnp.bfloat16)
    tables = (*lateral_tables(rows, cols), *lateral_tables(crows, ccols), widen, narrow)
    pack, unpack = column_tables(comps * layers)
    lat = pltpu.VMEM((2, comps, 256, cols), f32)
    tr, sh = fine_traction, coarse_shear

    uf, uc = fine_field, coarse_field
    ends = [pltpu.VMEM((*x.shape[:2], 8, x.shape[3]), f32) for x in (uf, uf, uc, uc)]
    x_down, x_up, pack = call(
        rows_kernel, (uf, uc, pack), [*edge_outs[:2], pltpu.VMEM(pack.shape, pack.dtype)],
        scratch=[*ends, pltpu.SemaphoreType.DMA((5,))], hbm=(0, 1, 2),
    )
    mine = (x_down, x_up, *call(columns_kernel, (uf, uc, pack), edge_outs[2:]))
    theirs = exchange(mine)
    sp, me, cs = fine_speed, fine_metric, coarse_speed
    vf, vc, *prep = call(
        functools.partial(main_kernel, True), (uf, sp, me, uc, cs, tr, *tables), [fine, coarse, *fixed_outs, *prep_outs],
        scratch=[lat, tall], flops=40_000_000,
    )
    vf, vc, change0, *mine = call(
        fix_kernel,
        (vf, vc, pack, unpack, uf, fine_previous, sp, me, uc, coarse_previous, cs, tr, sh, widen, narrow, *prep[:-1], *theirs),
        [fine, coarse, line] + edge_outs, scratch=[tall, corrections], alias={0: 0, 1: 1}, flops=20_000_000,
    )
    pf, pc, uf, uc, fixed = uf, uc, vf, vc, prep[: len(fixed_outs)]
    theirs = exchange(mine)
    vf, vc, *prep = call(
        functools.partial(main_kernel, False), (uf, sp, me, uc, cs, tr, *tables, *fixed, pf, pc),
        [fine, coarse, *prep_outs],
        scratch=[lat, tall], flops=40_000_000,
    )
    n = lax.axis_size(ALL)
    out_f, out_c, spread = call(
        last_kernel,
        (change0, unpack, sp, me, cs, uf, uc, vf, vc, tr, sh, widen, narrow, *fixed, *prep[:-1], *theirs),
        [pltpu.HBM(fine_field.shape, f32), pltpu.HBM(coarse_field.shape, f32), pltpu.VMEM((n, STEPS, 4), f32)],
        scratch=[fine, coarse, tall, corrections, pltpu.SemaphoreType.DMA((layers + 1,))], flops=40_000_000,
    )
    return out_f, out_c, jnp.max(lax.all_to_all(spread, ALL, 0, 0, tiled=True), axis=0)


def solution(mesh):
    field = P(None, None, "gx", Y)
    layered = P(None, "gx", Y)
    plane = P("gx", Y)
    return jax.shard_map(
        on_device,
        mesh=mesh,
        in_specs=(field, field, layered, layered, field, field, layered, plane, plane),
        out_specs=(field, field, P()),
        check_vma=False,
    )
```
